256 devices in a mesh: row: 32 (over z, x), col: 8 (over y, core).
Axes of the slice: x: 4, y: 4, z: 8, core: 2. Of those that a mesh axis runs over, the one named last changes fastest.
Arguments:
- hamiltonian: float32 [16384, 16384], P('row', 'col'), may hold values from -64 to 64, as said below
Outputs:
- updated: float32 [16384, 16384], P('row', 'col')
The draws below stay inside these ranges and needn't reach their ends.
Inputs may be any that keep to these rules, and one draw needn't show every extreme that they name: hamiltonian is symmetric as a matrix in natural order.
All inputs are finite; a program needn't handle non-finite values.
Results may differ from the reference program's by a relative error of at most 0.0001.
Values sent between devices are 32-bit elements; how exact they have to be, the bound alone decides.
A program may use at most 64 MiB of HBM per device.

```python
import jax
import jax.numpy as jnp
from jax import lax

N = 16384
NB = 128
PANELS = 2
GRID_ROWS = 32
GRID_COLS = 8


def draw_hamiltonian(key, part):
    first = jax.random.fold_in(jax.random.fold_in(key, 11), 0)
    raw = jnp.clip(jax.random.normal(first, (N, N), jnp.float32), -5.0, 5.0)
    blocks = jnp.arange(N) // NB
    scale = 0.5 + (blocks % GRID_ROWS).astype(jnp.float32) / max(GRID_ROWS - 1, 1)
    symmetric = (raw + raw.T) * 0.7071 * scale[:, None] * scale[None, :]
    shaped = symmetric.reshape(N // (GRID_ROWS * NB), GRID_ROWS, NB, N // (GRID_COLS * NB), GRID_COLS, NB)
    return shaped.transpose(1, 0, 2, 4, 3, 5).reshape(N, N)


def setup_inputs(seed: int = 0) -> dict:
    seeds = jax.random.split(jax.random.key(seed), 2)
    return {
        "hamiltonian": draw_hamiltonian(jax.random.fold_in(seeds[1], 71), 0),
    }


HIGH = lax.Precision.HIGHEST

def to_natural(matrix):
    shaped = matrix.reshape(GRID_ROWS, N // (GRID_ROWS * NB), NB, GRID_COLS, N // (GRID_COLS * NB), NB)
    return shaped.transpose(1, 0, 2, 4, 3, 5).reshape(N, N)

def to_stored(matrix):
    shaped = matrix.reshape(N // (GRID_ROWS * NB), GRID_ROWS, NB, N // (GRID_COLS * NB), GRID_COLS, NB)
    return shaped.transpose(1, 0, 2, 4, 3, 5).reshape(N, N)

def panel_step(matrix, panel):
    start = panel * NB
    position = jnp.arange(N)
    columns = matrix[:, start:start + NB]
    columns = jnp.where((position >= start + NB)[:, None], columns, jnp.float32(0.0))
    gram = jnp.dot(columns.T, columns, precision=HIGH)
    factor = jnp.linalg.cholesky(gram)
    reflect = lax.linalg.triangular_solve(factor, columns, left_side=False, lower=True, transpose_a=True)
    product = jnp.dot(matrix, reflect, precision=HIGH)
    coupling = jnp.dot(reflect.T, product, precision=HIGH)
    update = 2.0 * product - 2.0 * jnp.dot(reflect, coupling, precision=HIGH)
    return matrix - jnp.dot(reflect, update.T, precision=HIGH) - jnp.dot(update, reflect.T, precision=HIGH)

def reference(hamiltonian):
    matrix = to_natural(hamiltonian)
    for panel in range(PANELS):
        matrix = panel_step(matrix, panel)
    return to_stored(matrix)
```

```python
import functools

import jax
import jax.numpy as jnp
from jax import lax
from jax.experimental import pallas as pl
from jax.experimental.pallas import tpu as pltpu
from jax.sharding import PartitionSpec as P

NB = 128
Z, X, C = 8, 4, 8
SH = 64
MESH = pl.DeviceIdType.MESH
HIGH = lax.Precision.HIGHEST
F32 = jnp.float32


def dot(a, b):
    return lax.dot_general(a, b, (((1,), (0,)), ((), ())), precision=HIGH, preferred_element_type=F32)


def dot_nt(a, b):
    return lax.dot_general(a, b, (((1,), (1,)), ((), ())), precision=HIGH, preferred_element_type=F32)


def sweep_steps(a, groups):
    lane = lax.broadcasted_iota(jnp.int32, (NB, NB), 1)
    sub = lax.broadcasted_iota(jnp.int32, (NB, NB), 0)
    lane_row = lax.broadcasted_iota(jnp.int32, (1, NB), 1)

    def group(_, a):
        for t in range(8):
            pivot = 1.0 / a[t : t + 1, t : t + 1]
            row = a[t : t + 1, :] * pivot
            row = jnp.where(lane_row == t, pivot, row)
            column = jnp.broadcast_to(a[:, t : t + 1], (NB, NB))
            column = jnp.where(sub == t, -1.0, column)
            a = jnp.where((lane == t) | (sub == t), 0.0, a) - column * row
        a = pltpu.roll(a, NB - 8, 0)
        return pltpu.roll(a, NB - 8, 1)

    return lax.fori_loop(0, groups, group, a)


def kernel(
    h_hbm, lhs_ref, rhs_ref,
    hv, sh, col_form, row_form, part, rsb, ysh, p2c, stack, gsum, eb, gram, inv, sc1, sc2,
    h_sem, loc_sem, sc_send, sc_recv, ra_send, ra_recv, sp_send, sp_recv,
    rp_send, rp_recv, rs_send, rs_recv, es_send, es_recv, ea_send, ea_recv,
):
    r = lax.axis_index("row")
    c = lax.axis_index("col")
    z = r // X
    x = lax.rem(r, X)
    plane = lax.rem(r, C)
    rel = lax.rem(c - plane + C, C)
    z_up = lax.rem(z + 1, Z)
    z_down = lax.rem(z + Z - 1, Z)
    z_to = jnp.where(rel < 4, z_up, z)
    half = c // 4
    same = lax.rem(z, 2) == half
    z_from = jnp.where(same, z, z_down)

    def remote(src, dst, send, recv, row, col):
        return pltpu.make_async_remote_copy(
            src_ref=src, dst_ref=dst, send_sem=send, recv_sem=recv,
            device_id=(row, col), device_id_type=MESH,
        )

    def other(d):
        return lax.rem(c + d, C)

    started = []

    def go(copy):
        copy.start()
        started.append(copy)

    copy_h = pltpu.make_async_copy(h_hbm, hv, h_sem)
    copy_h.start()

    barrier = pltpu.get_barrier_semaphore()

    def greet(row, col):
        pl.semaphore_signal(barrier, inc=1, device_id=(row, col), device_id_type=MESH)

    for d in range(1, C):
        greet(r, other(d))
    for i in range(4):
        greet(z_to * X + i, plane)
        greet(z_from * X + lax.rem(c, X), lax.rem(c + jnp.where(same, 4, 0) + i, C))
    greet(z_up * X + x, c)
    greet(z_down * X + x, c)
    pl.semaphore_wait(barrier, 17)

    def mine(ref):
        return ref.at[pl.ds(pl.multiple_of(SH * c, SH), SH)]

    def scatter(v):
        def from_root(d):
            rows = pl.ds(pl.multiple_of(SH * other(d), SH), SH)
            return remote(h_hbm.at[rows, 0:NB], sh.at[v], sc_send.at[v, d], sc_recv.at[v], r, other(d))

        def own():
            rows = pl.ds(pl.multiple_of(SH * c, SH), SH)
            return pltpu.make_async_copy(h_hbm.at[rows, 0:NB], sh.at[v], loc_sem.at[v])

        @pl.when(c == v)
        def _():
            own().start()
            for d in range(1, C):
                from_root(d).start()

        def finish():
            @pl.when(c == v)
            def _():
                own().wait()
                for d in range(1, C):
                    from_root(d).wait_send()

            @pl.when(c != v)
            def _():
                from_root(1).wait_recv()

        return finish

    my_off = pl.multiple_of(((c // 2) * 4 + r // C) * NB + lax.rem(c, 2) * SH, SH)

    def distribute(v, shard):
        def send_rows():
            for d in range(1, C):
                go(remote(shard, mine(row_form.at[v]), ra_send.at[v, d], ra_recv.at[v, c], r, other(d)))
            row_form[v, pl.ds(pl.multiple_of(SH * c, SH), SH), :] = shard[...]

        for i in range(X):
            to = lax.rem(x + i, X)
            go(remote(
                shard, col_form.at[v, pl.ds(my_off, SH)],
                sp_send.at[v, i], sp_recv.at[v, lax.rem(rel, 4)], z_to * X + to, plane,
            ))
        send_rows()

    def wait_rows(v):
        for d in range(1, C):
            rows = pl.ds(pl.multiple_of(SH * other(d), SH), SH)
            remote(row_form.at[v, rows], row_form.at[v, rows], ra_send.at[v, d], ra_recv.at[v, other(d)], r, other(d)).wait_recv()

    def piece(v, block, i):
        aligned = lax.rem(block, 2) == half
        source = jnp.where(aligned, block, lax.rem(block + Z - 1, Z))
        sender = lax.rem(c + jnp.where(aligned, 4, 0) + i, C)
        off = ((sender // 2) * 4 + source // 2) * NB + lax.rem(sender, 2) * SH
        return col_form.at[v, pl.ds(pl.multiple_of(off, SH), SH)]

    def pieces(s, up):
        if s < 4:
            return range(4)
        return range(0, 2) if up else range(2, 4)

    def ring_copy(v, s, i, up, block):
        k = 0 if up else 1
        to = z_up if up else z_down
        ref = piece(v, block, i)
        return remote(ref, ref, rp_send.at[v, k, s - 1, i], rp_recv.at[v, k, s - 1, i], to * X + x, c)

    def ring_wait_piece(v, s, i, up):
        if s == 0:
            ref = piece(v, z, i)
            remote(ref, ref, sp_send.at[v, 0], sp_recv.at[v, i], r, c).wait_recv()
            return
        block = lax.rem(z - s + Z, Z) if up else lax.rem(z + s, Z)
        ring_copy(v, s, i, up, block).wait_recv()

    def ring(v, s):
        for i in range(4):
            if s == 1:
                ring_wait_piece(v, 0, i, True)
            for up in (True, False):
                if i not in pieces(s, up):
                    continue
                if s > 1:
                    ring_wait_piece(v, s - 1, i, up)
                block = lax.rem(z - (s - 1) + Z, Z) if up else lax.rem(z + s - 1, Z)
                go(ring_copy(v, s, i, up, block))

    def ring_end(v):
        for up in (True, False):
            for i in range(4):
                if i not in pieces(4, up):
                    ring_wait_piece(v, 3, i, up)
            for i in pieces(4, up):
                ring_wait_piece(v, 4, i, up)

    def reduce_start(q):
        for d in range(1, C):
            rows = pl.ds(pl.multiple_of(SH * other(d), SH), SH)
            go(remote(part.at[q, rows], rsb.at[q, d - 1], rs_send.at[q, d], rs_recv.at[q, d], r, other(d)))

    def reduce_end(q):
        total = part[q, pl.ds(pl.multiple_of(SH * c, SH), SH), :]
        for d in range(1, C):
            remote(rsb.at[q, d - 1], rsb.at[q, d - 1], rs_send.at[q, d], rs_recv.at[q, d], r, other(d)).wait_recv()
            total = total + rsb[q, d - 1]
        return total

    def exchange_start(e, rows):
        m = rows // C
        for d in range(1, C):
            src = stack.at[e, pl.ds(pl.multiple_of(m * other(d), 8), m)]
            go(remote(src, eb.at[e, d - 1, pl.ds(0, m)], es_send.at[e, d], es_recv.at[e, d], r, other(d)))

    def exchange_mid(e, rows):
        m = rows // C
        own = pl.ds(pl.multiple_of(m * c, 8), m)
        total = stack[e, own, :]
        for d in range(1, C):
            dst = eb.at[e, d - 1, pl.ds(0, m)]
            remote(dst, dst, es_send.at[e, d], es_recv.at[e, d], r, other(d)).wait_recv()
            total = total + eb[e, d - 1, pl.ds(0, m), :]
        gsum[e, own, :] = total
        for d in range(1, C):
            ref = gsum.at[e, own]
            go(remote(ref, ref, ea_send.at[e, d], ea_recv.at[e, c], r, other(d)))

    def exchange_end(e, rows):
        m = rows // C
        for d in range(1, C):
            ref = gsum.at[e, pl.ds(pl.multiple_of(m * other(d), 8), m)]
            remote(ref, ref, ea_send.at[e, d], ea_recv.at[e, other(d)], r, other(d)).wait_recv()

    def times_h(q, src):
        @pl.loop(0, 4)
        def _(j):
            rows = pl.ds(pl.multiple_of(j * NB, NB), NB)
            part[q, rows, :] = dot(hv[rows, :], src[...])

    def transpose_to(slot, src):
        @pl.loop(0, 16)
        def _(k):
            cols = pl.ds(pl.multiple_of(k * NB, NB), NB)
            rhs_ref[slot * NB : (slot + 1) * NB, cols] = src[cols, :].T

    eye = lax.broadcasted_iota(jnp.int32, (NB, NB), 0) == lax.broadcasted_iota(jnp.int32, (NB, NB), 1)

    def scaled(q):
        diagonal = jnp.where(eye, gram[q], 0.0)
        sc1[q] = jnp.broadcast_to(lax.rsqrt(jnp.sum(diagonal, axis=0, keepdims=True)), (NB, NB))
        sc2[q] = jnp.broadcast_to(lax.rsqrt(jnp.sum(diagonal, axis=1, keepdims=True)), (NB, NB))
        inv[q] = gram[q] * sc1[q] * sc2[q]

    def sweep(q, groups):
        inv[q] = sweep_steps(inv[q], groups)

    PV, CV, YV, UV = 0, 1, 2, 3
    finish_p = scatter(PV)
    finish_c = scatter(CV)
    finish_p()

    @pl.when((r == 0) & (c < 2))
    def _():
        sh[PV] = jnp.zeros((SH, NB), F32)

    distribute(PV, sh.at[PV])
    finish_c()
    distribute(CV, sh.at[CV])
    for s in range(1, 5):
        ring(PV, s)
    ring_end(PV)
    ring(CV, 1)
    copy_h.wait()
    times_h(0, col_form.at[PV])
    reduce_start(0)
    ring(CV, 2)
    transpose_to(1, col_form.at[PV])
    stack[0, 0:NB, :] = dot(rhs_ref[NB : 2 * NB, :], col_form[PV])
    stack[0, NB : 2 * NB, :] = jnp.where(c == 1, col_form[PV, 0:NB, :], 0.0)
    exchange_start(0, 2 * NB)
    ysh[0] = reduce_end(0)
    distribute(YV, ysh.at[0])
    exchange_mid(0, 2 * NB)
    ring(CV, 3)
    ring(YV, 1)
    exchange_end(0, 2 * NB)
    gram[0] = gsum[0, 0:NB, :]
    scaled(0)
    sweep(0, 5)
    ring(CV, 4)
    ring(YV, 2)
    sweep(0, 5)
    ring(YV, 3)
    sweep(0, 6)
    ring(YV, 4)
    ring_end(CV)
    wait_rows(PV)
    wait_rows(CV)
    wait_rows(YV)
    ring_end(YV)
    transpose_to(0, col_form.at[YV])
    stack[1, 0:NB, :] = dot(rhs_ref[NB : 2 * NB, :], col_form[YV])
    stack[1, NB : 2 * NB, :] = jnp.where(c == 1, col_form[YV, 0:NB, :], 0.0)
    exchange_start(1, 2 * NB)
    exchange_mid(1, 2 * NB)
    exchange_end(1, 2 * NB)
    k1, d1, e1 = inv[0], sc1[0], sc2[0]
    s1 = gsum[1, 0:NB, :] * d1 * e1

    def factors(p, y, k, s, d):
        pk = dot(p * d[0:1, :], k)
        alpha = -2.0 * pk * d[0:1, :]
        beta = dot(4.0 * dot(pk, s) - 2.0 * (y * d[0:1, :]), k) * d[0:1, :]
        return alpha, beta

    alpha_b, beta_b = factors(gsum[0, NB : 2 * NB, :], gsum[1, NB : 2 * NB, :], k1, s1, d1)
    sub = lax.broadcasted_iota(jnp.int32, (NB, NB), 0)

    @pl.loop(0, 16)
    def _(k):
        rows = pl.ds(pl.multiple_of(k * NB, NB), NB)
        value = (
            col_form[CV, rows, :]
            + dot_nt(col_form[YV, rows, :], alpha_b)
            + dot_nt(col_form[PV, rows, :], beta_b)
        )
        p2c[rows, :] = jnp.where((k == 0) & (c < 2), 0.0, value)

    times_h(1, p2c)
    reduce_start(1)
    transpose_to(3, p2c)
    stack[2, 0:NB, :] = dot(rhs_ref[3 * NB : 4 * NB, :], p2c[...])
    stack[2, NB : 2 * NB, :] = dot(rhs_ref[0:NB, :], p2c[...])
    stack[2, 2 * NB : 3 * NB, :] = dot(rhs_ref[NB : 2 * NB, :], p2c[...])
    exchange_start(2, 3 * NB)
    ysh[1] = reduce_end(1)
    distribute(UV, ysh.at[1])
    exchange_mid(2, 3 * NB)
    ring(UV, 1)
    exchange_end(2, 3 * NB)
    gram[1] = gsum[2, 0:NB, :]
    scaled(1)
    sweep(1, 5)
    ring(UV, 2)
    sweep(1, 5)
    ring(UV, 3)
    sweep(1, 6)
    ring(UV, 4)
    t1, t2 = gsum[2, NB : 2 * NB, :], gsum[2, 2 * NB : 3 * NB, :]
    kt2 = dot(k1, t2 * e1)
    a = -2.0 * kt2 * e1
    b = dot(k1, 4.0 * dot(s1, kt2) - 2.0 * (t1 * e1)) * e1
    wait_rows(UV)
    ring_end(UV)
    transpose_to(2, col_form.at[UV])
    stack[3, 0:NB, :] = dot(rhs_ref[3 * NB : 4 * NB, :], col_form[UV])
    exchange_start(3, NB)
    exchange_mid(3, NB)
    exchange_end(3, NB)
    k2, d2, e2 = inv[1], sc1[1], sc2[1]

    def dot_tn(left, right):
        return lax.dot_general(left, right, (((0,), (0,)), ((), ())), precision=HIGH, preferred_element_type=F32)

    s2 = (gsum[3, 0:NB, :] + dot_tn(t1, a) + dot_tn(t2, b)) * d2 * e2
    for j in range(4):
        rows = slice(j * NB, (j + 1) * NB)
        p1, c1, y1, u = (row_form[v, rows, :] for v in range(4))
        alpha1, beta1 = factors(p1, y1, k1, s1, d1)
        p2 = c1 + dot_nt(y1, alpha_b) + dot_nt(p1, beta_b)
        if j == 0:
            p2 = jnp.where(r < 2, 0.0, p2)
        y2 = u + dot(y1, a) + dot(p1, b)
        alpha2, beta2 = factors(p2, y2, k2, s2, d2)
        lhs_ref[rows, 0:NB] = alpha1 + dot_nt(alpha2, a)
        lhs_ref[rows, NB : 2 * NB] = beta1 + dot_nt(alpha2, b)
        lhs_ref[rows, 2 * NB : 3 * NB] = alpha2
        lhs_ref[rows, 3 * NB : 4 * NB] = beta2
    for copy in started:
        copy.wait_send()


def factors_kernel(hamiltonian):
    rows, cols = hamiltonian.shape
    dma = pltpu.SemaphoreType.DMA
    vmem = pl.BlockSpec(memory_space=pltpu.VMEM)
    return pl.pallas_call(
        kernel,
        out_shape=(
            jax.ShapeDtypeStruct((rows, 4 * NB), F32),
            jax.ShapeDtypeStruct((4 * NB, cols), F32),
        ),
        in_specs=[pl.BlockSpec(memory_space=pl.ANY)],
        out_specs=(vmem, vmem),
        scratch_shapes=[
            pltpu.VMEM((rows, cols), F32),
            pltpu.VMEM((2, SH, NB), F32),
            pltpu.VMEM((4, cols, NB), F32),
            pltpu.VMEM((4, rows, NB), F32),
            pltpu.VMEM((2, rows, NB), F32),
            pltpu.VMEM((2, C - 1, SH, NB), F32),
            pltpu.VMEM((2, SH, NB), F32),
            pltpu.VMEM((cols, NB), F32),
            pltpu.VMEM((4, 3 * NB, NB), F32),
            pltpu.VMEM((4, 3 * NB, NB), F32),
            pltpu.VMEM((4, C - 1, 3 * NB // C, NB), F32),
            pltpu.VMEM((2, NB, NB), F32),
            pltpu.VMEM((2, NB, NB), F32),
            pltpu.VMEM((2, NB, NB), F32),
            pltpu.VMEM((2, NB, NB), F32),
            dma, dma((2,)), dma((2, C)), dma((2,)),
            dma((4, C)), dma((4, C)), dma((4, 4)), dma((4, 4)),
            dma((4, 2, 4, 4)), dma((4, 2, 4, 4)),
            dma((2, C)), dma((2, C)),
            dma((4, C)), dma((4, C)), dma((4, C)), dma((4, C)),
        ],
        compiler_params=pltpu.CompilerParams(
            collective_id=0, has_side_effects=True, vmem_limit_bytes=60 * 1024 * 1024
        ),
        name="reflector_factors",
    )(hamiltonian)


def update_kernel(h_ref, lhs_ref, rhs_ref, out_ref):
    out_ref[...] = h_ref[...] + dot(lhs_ref[...], rhs_ref[...])


def update(hamiltonian, lhs, rhs):
    rows, cols = hamiltonian.shape
    tile = 128
    return pl.pallas_call(
        update_kernel,
        grid=(rows // tile,),
        out_shape=jax.ShapeDtypeStruct((rows, cols), F32),
        in_specs=[
            pl.BlockSpec((tile, cols), lambda i: (i, 0)),
            pl.BlockSpec((tile, 4 * NB), lambda i: (i, 0)),
            pl.BlockSpec((4 * NB, cols), lambda i: (0, 0)),
        ],
        out_specs=pl.BlockSpec((tile, cols), lambda i: (i, 0)),
        compiler_params=pltpu.CompilerParams(vmem_limit_bytes=40 * 1024 * 1024),
        name="apply_factors",
    )(hamiltonian, lhs, rhs)


def body(hamiltonian):
    lhs, rhs = factors_kernel(hamiltonian)
    return update(hamiltonian, lhs, rhs)


def solution(mesh):
    return jax.shard_map(
        body, mesh=mesh, in_specs=(P("row", "col"),), out_specs=P("row", "col"), check_vma=False
    )
```

```python
import functools

import jax
import jax.numpy as jnp
from jax import lax
from jax.experimental import pallas as pl
from jax.experimental.pallas import tpu as pltpu
from jax.sharding import PartitionSpec as P

NB = 128
Z, X, C = 8, 4, 8
SH = 64
MESH = pl.DeviceIdType.MESH
HIGH = lax.Precision.HIGHEST
F32 = jnp.float32


def dot(a, b):
    return lax.dot_general(a, b, (((1,), (0,)), ((), ())), precision=HIGH, preferred_element_type=F32)


def dot_nt(a, b):
    return lax.dot_general(a, b, (((1,), (1,)), ((), ())), precision=HIGH, preferred_element_type=F32)


def dot_tn(a, b):
    return lax.dot_general(a, b, (((0,), (0,)), ((), ())), precision=HIGH, preferred_element_type=F32)


def sweep_steps(a, groups):
    lane = lax.broadcasted_iota(jnp.int32, (NB, NB), 1)
    sub = lax.broadcasted_iota(jnp.int32, (NB, NB), 0)
    lane_row = lax.broadcasted_iota(jnp.int32, (1, NB), 1)

    def group(_, a):
        for t in range(8):
            pivot = 1.0 / a[t : t + 1, t : t + 1]
            row = a[t : t + 1, :] * pivot
            row = jnp.where(lane_row == t, pivot, row)
            column = jnp.broadcast_to(a[:, t : t + 1], (NB, NB))
            column = jnp.where(sub == t, -1.0, column)
            a = jnp.where((lane == t) | (sub == t), 0.0, a) - column * row
        a = pltpu.roll(a, NB - 8, 0)
        return pltpu.roll(a, NB - 8, 1)

    return lax.fori_loop(0, groups, group, a)


def kernel(
    h_hbm, hv, lhs_ref, up,
    sh, yp, cform, ypr, cr, ur, p2r, ab1, part, rsb, ysh, abt, ab,
    pstack, xb, zb, gsum, inv, sc1, sc2,
    h_sem, loc_sem, sc_send, sc_recv, ra_send, ra_recv, sp_send, sp_recv,
    rp_send, rp_recv, rs_send, rs_recv, px_send, px_recv, pz_send, pz_recv, pc_send, pc_recv,
):
    r = lax.axis_index("row")
    c = lax.axis_index("col")
    z = r // X
    x = lax.rem(r, X)
    plane = lax.rem(r, C)
    rel = lax.rem(c - plane + C, C)
    z_up = lax.rem(z + 1, Z)
    z_down = lax.rem(z + Z - 1, Z)
    z_to = jnp.where(rel < 4, z_up, z)
    half = c // 4
    same = lax.rem(z, 2) == half
    z_from = jnp.where(same, z, z_down)

    def remote(src, dst, send, recv, row, col):
        return pltpu.make_async_remote_copy(
            src_ref=src, dst_ref=dst, send_sem=send, recv_sem=recv,
            device_id=(row, col), device_id_type=MESH,
        )

    def landed(ref, send, recv):
        remote(ref, ref, send, recv, r, c).wait_recv()

    def other(d):
        return lax.rem(c + d, C)

    started = []

    def go(copy):
        copy.start()
        started.append(copy)

    copy_h = pltpu.make_async_copy(h_hbm, hv, h_sem)
    copy_h.start()

    barrier = pltpu.get_barrier_semaphore()

    def greet(row, col):
        pl.semaphore_signal(barrier, inc=1, device_id=(row, col), device_id_type=MESH)

    for d in range(1, C):
        greet(r, other(d))
    for i in range(4):
        greet(z_to * X + i, plane)
        greet(z_from * X + lax.rem(c, X), lax.rem(c + jnp.where(same, 4, 0) + i, C))
    for d in range(1, X):
        greet(z * X + lax.rem(x + d, X), c)
    for d in range(1, Z):
        greet(lax.rem(z + d, Z) * X + x, c)
    pl.semaphore_wait(barrier, 25)

    PV, CV, YV, UV = 0, 1, 2, 3

    def column(v, rows):
        if v == CV:
            return cform.at[rows]
        if v == PV:
            return yp.at[rows, NB : 2 * NB]
        return (up if v == UV else yp).at[rows, 0:NB]

    def row(v, rows):
        if v == PV:
            return ypr.at[rows, NB : 2 * NB]
        if v == YV:
            return ypr.at[rows, 0:NB]
        return (cr if v == CV else ur).at[rows]

    def at(start, size):
        return pl.ds(pl.multiple_of(start, 8), size)

    def scatter(v):
        def from_root(d):
            return remote(h_hbm.at[at(SH * other(d), SH), 0:NB], sh.at[v], sc_send.at[v, d], sc_recv.at[v], r, other(d))

        def own():
            return pltpu.make_async_copy(h_hbm.at[at(SH * c, SH), 0:NB], sh.at[v], loc_sem.at[v])

        @pl.when(c == v)
        def _():
            own().start()
            for d in range(1, C):
                from_root(d).start()

        def finish():
            @pl.when(c == v)
            def _():
                own().wait()
                for d in range(1, C):
                    from_root(d).wait_send()

            @pl.when(c != v)
            def _():
                from_root(1).wait_recv()

        return finish

    my_off = ((c // 2) * 4 + r // C) * NB + lax.rem(c, 2) * SH

    def distribute(v, shard):
        for i in range(X):
            to = lax.rem(x + i, X)
            go(remote(
                shard, column(v, at(my_off, SH)),
                sp_send.at[v, i], sp_recv.at[v, lax.rem(rel, 4)], z_to * X + to, plane,
            ))
        mine = row(v, at(SH * c, SH))
        for d in range(1, C):
            go(remote(shard, mine, ra_send.at[v, d], ra_recv.at[v, c], r, other(d)))
        mine[...] = shard[...]

    def wait_rows(v):
        for d in range(1, C):
            landed(row(v, at(SH * other(d), SH)), ra_send.at[v, d], ra_recv.at[v, other(d)])

    def piece(v, block, i):
        aligned = lax.rem(block, 2) == half
        source = jnp.where(aligned, block, lax.rem(block + Z - 1, Z))
        sender = lax.rem(c + jnp.where(aligned, 4, 0) + i, C)
        return column(v, at(((sender // 2) * 4 + source // 2) * NB + lax.rem(sender, 2) * SH, SH))

    def pieces(s, up_way):
        if s < 4:
            return range(4)
        return range(0, 2) if up_way else range(2, 4)

    def ring_copy(v, s, i, up_way, block):
        k = 0 if up_way else 1
        to = z_up if up_way else z_down
        ref = piece(v, block, i)
        return remote(ref, ref, rp_send.at[v, k, s - 1, i], rp_recv.at[v, k, s - 1, i], to * X + x, c)

    def ring_wait_piece(v, s, i, up_way):
        if s == 0:
            landed(piece(v, z, i), sp_send.at[v, 0], sp_recv.at[v, i])
            return
        block = lax.rem(z - s + Z, Z) if up_way else lax.rem(z + s, Z)
        ring_copy(v, s, i, up_way, block).wait_recv()

    def ring(v, s):
        for i in range(4):
            if s == 1:
                ring_wait_piece(v, 0, i, True)
            for up_way in (True, False):
                if i not in pieces(s, up_way):
                    continue
                if s > 1:
                    ring_wait_piece(v, s - 1, i, up_way)
                block = lax.rem(z - (s - 1) + Z, Z) if up_way else lax.rem(z + s - 1, Z)
                go(ring_copy(v, s, i, up_way, block))

    def ring_end(v):
        for up_way in (True, False):
            for i in range(4):
                if i not in pieces(4, up_way):
                    ring_wait_piece(v, 3, i, up_way)
            for i in pieces(4, up_way):
                ring_wait_piece(v, 4, i, up_way)

    def reduce_start(q):
        for d in range(1, C):
            go(remote(part.at[q, at(SH * other(d), SH)], rsb.at[q, d - 1], rs_send.at[q, d], rs_recv.at[q, d], r, other(d)))

    def reduce_end(q):
        total = part[q, at(SH * c, SH), :]
        for d in range(1, C):
            landed(rsb.at[q, d - 1], rs_send.at[q, d], rs_recv.at[q, d])
            total = total + rsb[q, d - 1]
        ysh[q] = total

    sizes = (3 * NB, NB, 3 * NB, NB)

    def sum_start(e):
        m = sizes[e] // C
        xb[e, x, 0:m, :] = pstack[e, at(m * c, m), :]
        for d in range(1, X):
            go(remote(
                pstack.at[e, at(m * c, m)], xb.at[e, x, 0:m], px_send.at[e, d], px_recv.at[e, x],
                z * X + lax.rem(x + d, X), c,
            ))

    def sum_z(e):
        m = sizes[e] // C
        for d in range(1, X):
            k = lax.rem(x + d, X)
            landed(xb.at[e, k, 0:m], px_send.at[e, d], px_recv.at[e, k])
        zb[e, z, 0:m, :] = (xb[e, 0, 0:m, :] + xb[e, 1, 0:m, :]) + (xb[e, 2, 0:m, :] + xb[e, 3, 0:m, :])
        for d in range(1, Z):
            ref = zb.at[e, z, 0:m]
            go(remote(ref, ref, pz_send.at[e, d], pz_recv.at[e, z], lax.rem(z + d, Z) * X + x, c))

    def sum_col(e):
        m = sizes[e] // C
        for d in range(1, Z):
            k = lax.rem(z + d, Z)
            landed(zb.at[e, k, 0:m], pz_send.at[e, d], pz_recv.at[e, k])
        total = zb[e, 0, 0:m, :]
        for k in range(1, Z):
            total = total + zb[e, k, 0:m, :]
        gsum[e, at(m * c, m), :] = total
        for d in range(1, C):
            ref = gsum.at[e, at(m * c, m)]
            go(remote(ref, ref, pc_send.at[e, d], pc_recv.at[e, c], r, other(d)))

    def sum_end(e):
        m = sizes[e] // C
        for d in range(1, C):
            landed(gsum.at[e, at(m * other(d), m)], pc_send.at[e, d], pc_recv.at[e, other(d)])

    def times_h(q, src, first, last):
        @pl.loop(first, last)
        def _(j):
            rows = pl.ds(pl.multiple_of(j * NB, NB), NB)
            part[q, rows, :] = dot(hv[rows, :], src[...])

    eye = lax.broadcasted_iota(jnp.int32, (NB, NB), 0) == lax.broadcasted_iota(jnp.int32, (NB, NB), 1)

    def scaled(q, e):
        gram = gsum[e, 0:NB, :]
        diagonal = jnp.where(eye, gram, 0.0)
        sc1[q] = jnp.broadcast_to(lax.rsqrt(jnp.sum(diagonal, axis=0, keepdims=True)), (NB, NB))
        sc2[q] = jnp.broadcast_to(lax.rsqrt(jnp.sum(diagonal, axis=1, keepdims=True)), (NB, NB))
        inv[q] = gram * sc1[q] * sc2[q]

    def sweep(q, groups):
        inv[q] = sweep_steps(inv[q], groups)

    def factors(p, y, k, s, d):
        pk = dot(p * d[0:1, :], k)
        alpha = -2.0 * pk * d[0:1, :]
        beta = dot(4.0 * dot(pk, s) - 2.0 * (y * d[0:1, :]), k) * d[0:1, :]
        return alpha, beta

    finish_p = scatter(PV)
    finish_c = scatter(CV)
    finish_p()

    @pl.when((r == 0) & (c < 2))
    def _():
        sh[PV] = jnp.zeros((SH, NB), F32)

    distribute(PV, sh.at[PV])
    finish_c()
    distribute(CV, sh.at[CV])
    ring(PV, 1)
    wait_rows(PV)
    wait_rows(CV)
    p1 = ypr[:, NB : 2 * NB]
    pstack[0, 0:NB, :] = dot_tn(p1, p1)
    pstack[0, NB : 2 * NB, :] = dot_tn(cr[...], p1)
    pstack[0, 2 * NB : 3 * NB, :] = jnp.where(r == 1, ypr[0:NB, NB : 2 * NB], 0.0)
    sum_start(0)
    ring(PV, 2)
    sum_z(0)
    ring(PV, 3)
    ring(PV, 4)
    sum_col(0)
    ring_end(PV)
    ring(CV, 1)
    copy_h.wait()
    times_h(0, column(PV, slice(None)), 0, 2)
    ring(CV, 2)
    times_h(0, column(PV, slice(None)), 2, 4)
    reduce_start(0)
    sum_end(0)
    scaled(0, 0)
    sweep(0, 3)
    ring(CV, 3)
    sweep(0, 2)
    reduce_end(0)
    distribute(YV, ysh.at[0])
    ring(CV, 4)
    sweep(0, 4)
    ring(YV, 1)
    wait_rows(YV)
    pstack[1, 0:NB, :] = dot_tn(ypr[:, NB : 2 * NB], ypr[:, 0:NB])
    sum_start(1)
    sweep(0, 3)
    ring(YV, 2)
    sum_z(1)
    sweep(0, 4)
    ring(YV, 3)
    sum_col(1)
    ring(YV, 4)
    sum_end(1)
    k1, d1, e1 = inv[0], sc1[0], sc2[0]
    s1 = gsum[1, 0:NB, :] * d1 * e1
    alpha_b, beta_b = factors(gsum[0, 2 * NB : 3 * NB, :], gsum[0, NB : 2 * NB, :], k1, s1, d1)
    abt[0:NB, :] = alpha_b.T
    abt[NB : 2 * NB, :] = beta_b.T
    p2r[...] = cr[...] + dot(ypr[...], abt[...])

    @pl.when(r < 2)
    def _():
        p2r[0:NB, :] = jnp.zeros((NB, NB), F32)

    pstack[2, 0:NB, :] = dot_tn(p2r[...], p2r[...])
    pstack[2, NB : 3 * NB, :] = dot_tn(ypr[...], p2r[...])
    sum_start(2)
    ring_end(CV)
    ring_end(YV)

    @pl.loop(0, 16)
    def _(k):
        rows = pl.ds(pl.multiple_of(k * NB, NB), NB)
        value = cform[rows, :] + dot(yp[rows, :], abt[...])
        up[rows, NB : 2 * NB] = jnp.where((k == 0) & (c < 2), 0.0, value)

    sum_z(2)
    times_h(1, up.at[:, NB : 2 * NB], 0, 4)
    reduce_start(1)
    sum_col(2)
    alpha1, beta1 = factors(ypr[:, NB : 2 * NB], ypr[:, 0:NB], k1, s1, d1)
    ab1[:, 0:NB] = alpha1
    ab1[:, NB : 2 * NB] = beta1
    reduce_end(1)
    distribute(UV, ysh.at[1])
    sum_end(2)
    scaled(1, 2)
    sweep(1, 4)
    ring(UV, 1)
    wait_rows(UV)
    pstack[3, 0:NB, :] = dot_tn(p2r[...], ur[...])
    sum_start(3)
    sweep(1, 3)
    ring(UV, 2)
    sum_z(3)
    sweep(1, 4)
    ring(UV, 3)
    sum_col(3)
    sweep(1, 5)
    ring(UV, 4)
    k2, d2, e2 = inv[1], sc1[1], sc2[1]
    t1, t2 = gsum[2, NB : 2 * NB, :], gsum[2, 2 * NB : 3 * NB, :]
    kt2 = dot(k1, t2 * e1)
    ab[0:NB, :] = -2.0 * kt2 * e1
    ab[NB : 2 * NB, :] = dot(k1, 4.0 * dot(s1, kt2) - 2.0 * (t1 * e1)) * e1
    pk2 = dot(p2r[...] * d2[0:1, :], k2)
    alpha2 = -2.0 * pk2 * d2[0:1, :]
    lhs_ref[:, 0:NB] = alpha2
    ab1[...] = ab1[...] + dot_nt(alpha2, ab[...])
    y2 = ur[...] + dot(ypr[...], ab[...])

    @pl.loop(0, 8)
    def _(k):
        cols = pl.ds(pl.multiple_of(k * 2 * NB, 2 * NB), 2 * NB)
        hv[:, cols] = hv[:, cols] + dot_nt(ab1[...], yp[cols, :])

    sum_end(3)
    s2 = (gsum[3, 0:NB, :] + dot_tn(gsum[2, NB : 3 * NB, :], ab[...])) * d2 * e2
    lhs_ref[:, NB : 2 * NB] = dot(4.0 * dot(pk2, s2) - 2.0 * (y2 * d2[0:1, :]), k2) * d2[0:1, :]
    ring_end(UV)
    for copy in started:
        copy.wait_send()


def factors_kernel(hamiltonian):
    rows, cols = hamiltonian.shape
    dma = pltpu.SemaphoreType.DMA
    vmem = pl.BlockSpec(memory_space=pltpu.VMEM)
    return pl.pallas_call(
        kernel,
        out_shape=(
            pltpu.VMEM((rows, cols), F32),
            pltpu.VMEM((rows, 2 * NB), F32),
            pltpu.VMEM((cols, 2 * NB), F32),
        ),
        in_specs=[pl.BlockSpec(memory_space=pltpu.HBM)],
        out_specs=(vmem, vmem, vmem),
        scratch_shapes=[
            pltpu.VMEM((2, SH, NB), F32),
            pltpu.VMEM((cols, 2 * NB), F32),
            pltpu.VMEM((cols, NB), F32),
            pltpu.VMEM((rows, 2 * NB), F32),
            pltpu.VMEM((rows, NB), F32),
            pltpu.VMEM((rows, NB), F32),
            pltpu.VMEM((rows, NB), F32),
            pltpu.VMEM((rows, 2 * NB), F32),
            pltpu.VMEM((2, rows, NB), F32),
            pltpu.VMEM((2, C - 1, SH, NB), F32),
            pltpu.VMEM((2, SH, NB), F32),
            pltpu.VMEM((2 * NB, NB), F32),
            pltpu.VMEM((2 * NB, NB), F32),
            pltpu.VMEM((4, 3 * NB, NB), F32),
            pltpu.VMEM((4, X, 3 * NB // C, NB), F32),
            pltpu.VMEM((4, Z, 3 * NB // C, NB), F32),
            pltpu.VMEM((4, 3 * NB, NB), F32),
            pltpu.VMEM((2, NB, NB), F32),
            pltpu.VMEM((2, NB, NB), F32),
            pltpu.VMEM((2, NB, NB), F32),
            dma, dma((2,)), dma((2, C)), dma((2,)),
            dma((4, C)), dma((4, C)), dma((4, 4)), dma((4, 4)),
            dma((4, 2, 4, 4)), dma((4, 2, 4, 4)),
            dma((2, C)), dma((2, C)),
            dma((4, X)), dma((4, X)), dma((4, Z)), dma((4, Z)), dma((4, C)), dma((4, C)),
        ],
        compiler_params=pltpu.CompilerParams(
            collective_id=0, has_side_effects=True, vmem_limit_bytes=32 * 1024 * 1024
        ),
        name="reflector_factors",
    )(hamiltonian)


def update_kernel(h_ref, lhs_ref, up_ref, out_ref):
    cols = pl.ds(pl.multiple_of(pl.program_id(0) * 2 * NB, 2 * NB), 2 * NB)
    out_ref[...] = h_ref[:, cols] + dot_nt(lhs_ref[...], up_ref[cols, :])


def update(partly, lhs, up):
    rows, cols = partly.shape
    vmem = pl.BlockSpec(memory_space=pltpu.VMEM)
    return pl.pallas_call(
        update_kernel,
        grid=(cols // (2 * NB),),
        out_shape=jax.ShapeDtypeStruct((rows, cols), F32),
        in_specs=[vmem, vmem, vmem],
        out_specs=pl.BlockSpec((rows, 2 * NB), lambda i: (0, i)),
        compiler_params=pltpu.CompilerParams(vmem_limit_bytes=24 * 1024 * 1024),
        name="apply_factors",
    )(partly, lhs, up)


def body(hamiltonian):
    return update(*factors_kernel(pltpu.with_memory_space_constraint(hamiltonian, pltpu.HBM)))


def solution(mesh):
    return jax.shard_map(
        body, mesh=mesh, in_specs=(P("row", "col"),), out_specs=P("row", "col"), check_vma=False
    )
```

```python
import functools

import jax
import jax.numpy as jnp
from jax import lax
from jax.experimental import pallas as pl
from jax.experimental.pallas import tpu as pltpu
from jax.sharding import PartitionSpec as P

NB = 128
Z, X, C = 8, 4, 8
SH = 64
MESH = pl.DeviceIdType.MESH
HIGH = lax.Precision.HIGHEST
F32 = jnp.float32
BF16 = jnp.bfloat16


def dot(a, b):
    return lax.dot_general(a, b, (((1,), (0,)), ((), ())), precision=HIGH, preferred_element_type=F32)


def dot_nt(a, b):
    return lax.dot_general(a, b, (((1,), (1,)), ((), ())), precision=HIGH, preferred_element_type=F32)


def dot_tn(a, b):
    return lax.dot_general(a, b, (((0,), (0,)), ((), ())), precision=HIGH, preferred_element_type=F32)


def dot_b(a, b, contract):
    return lax.dot_general(a, b, (contract, ((), ())), preferred_element_type=F32)


def halves(value):
    high = value.astype(BF16)
    return high, (value - high.astype(F32)).astype(BF16)


def sweep_steps(a, groups):
    tile = (8, NB)
    lane = lax.broadcasted_iota(jnp.int32, tile, 1)
    sub = lax.broadcasted_iota(jnp.int32, tile, 0)

    def group(_, a):
        for t in range(0, 8, 2):
            r0 = jnp.broadcast_to(a[0, t : t + 1, :], tile)
            r1 = jnp.broadcast_to(a[0, t + 1 : t + 2, :], tile)
            p = jnp.broadcast_to(r0[:, t : t + 1], tile)
            q = jnp.broadcast_to(r0[:, t + 1 : t + 2], tile)
            s = jnp.broadcast_to(r1[:, t + 1 : t + 2], tile)
            scale = 1.0 / (p * s - q * q)
            i00, i01, i11 = s * scale, -q * scale, p * scale
            n0 = jnp.where(lane == t, i00, jnp.where(lane == t + 1, i01, i00 * r0 + i01 * r1))
            n1 = jnp.where(lane == t, i01, jnp.where(lane == t + 1, i11, i01 * r0 + i11 * r1))
            c0 = jnp.broadcast_to(a[:, :, t : t + 1], a.shape)
            c1 = jnp.broadcast_to(a[:, :, t + 1 : t + 2], a.shape)
            pivot_lane = ((lane == t) | (lane == t + 1))[None]
            rest = jnp.where(pivot_lane, 0.0, a) - c0 * n0[None] - c1 * n1[None]
            top = jnp.where(sub == t, n0, jnp.where(sub == t + 1, n1, rest[0]))
            a = jnp.concatenate([top[None], rest[1:]], axis=0)
        a = jnp.concatenate([a[1:], a[:1]], axis=0)
        return pltpu.roll(a, NB - 8, 2)

    return lax.fori_loop(0, groups, group, a.reshape(NB // 8, 8, NB)).reshape(NB, NB)


def kernel(
    h_hbm, hv, lhs_ref, up,
    sh, yp, cform, ypr, cr, ur, p2r, ab1, part, rsb, ysh, abt, ab,
    pstack, xb, zb, gsum, inv, sc1, sc2, hh, hl, vs, abts, abh,
    h_sem, loc_sem, sc_send, sc_recv, ra_send, ra_recv, sp_send, sp_recv,
    rp_send, rp_recv, rs_send, rs_recv, px_send, px_recv, pz_send, pz_recv, pc_send, pc_recv,
):
    r = lax.axis_index("row")
    c = lax.axis_index("col")
    z = r // X
    x = lax.rem(r, X)
    plane = lax.rem(r, C)
    rel = lax.rem(c - plane + C, C)
    z_up = lax.rem(z + 1, Z)
    z_down = lax.rem(z + Z - 1, Z)
    z_to = jnp.where(rel < 4, z_up, z)
    half = c // 4
    same = lax.rem(z, 2) == half
    z_from = jnp.where(same, z, z_down)

    def remote(src, dst, send, recv, row, col):
        return pltpu.make_async_remote_copy(
            src_ref=src, dst_ref=dst, send_sem=send, recv_sem=recv,
            device_id=(row, col), device_id_type=MESH,
        )

    def landed(ref, send, recv):
        remote(ref, ref, send, recv, r, c).wait_recv()

    def other(d):
        return lax.rem(c + d, C)

    started = []

    def go(copy):
        copy.start()
        started.append(copy)

    copy_h = pltpu.make_async_copy(h_hbm, hv, h_sem)
    copy_h.start()

    barrier = pltpu.get_barrier_semaphore()

    def greet(row, col):
        pl.semaphore_signal(barrier, inc=1, device_id=(row, col), device_id_type=MESH)

    for d in range(1, C):
        greet(r, other(d))
    for i in range(4):
        greet(z_to * X + i, plane)
        greet(z_from * X + lax.rem(c, X), lax.rem(c + jnp.where(same, 4, 0) + i, C))
    for d in range(1, X):
        greet(z * X + lax.rem(x + d, X), c)
    for d in range(1, Z):
        greet(lax.rem(z + d, Z) * X + x, c)
    pl.semaphore_wait(barrier, 25)

    PV, CV, YV, UV = 0, 1, 2, 3

    def column(v, rows):
        if v == CV:
            return cform.at[rows]
        if v == PV:
            return yp.at[rows, NB : 2 * NB]
        return (up if v == UV else yp).at[rows, 0:NB]

    def row(v, rows):
        if v == PV:
            return ypr.at[rows, NB : 2 * NB]
        if v == YV:
            return ypr.at[rows, 0:NB]
        return (cr if v == CV else ur).at[rows]

    def at(start, size):
        return pl.ds(pl.multiple_of(start, 8), size)

    def scatter(v):
        def from_root(d):
            return remote(h_hbm.at[at(SH * other(d), SH), 0:NB], sh.at[v], sc_send.at[v, d], sc_recv.at[v], r, other(d))

        def own():
            return pltpu.make_async_copy(h_hbm.at[at(SH * c, SH), 0:NB], sh.at[v], loc_sem.at[v])

        @pl.when(c == v)
        def _():
            own().start()
            for d in range(1, C):
                from_root(d).start()

        def finish():
            @pl.when(c == v)
            def _():
                own().wait()
                for d in range(1, C):
                    from_root(d).wait_send()

            @pl.when(c != v)
            def _():
                from_root(1).wait_recv()

        return finish

    my_off = ((c // 2) * 4 + r // C) * NB + lax.rem(c, 2) * SH

    def distribute(v, shard):
        for i in range(X):
            to = lax.rem(x + i, X)
            go(remote(
                shard, column(v, at(my_off, SH)),
                sp_send.at[v, i], sp_recv.at[v, lax.rem(rel, 4)], z_to * X + to, plane,
            ))
        mine = row(v, at(SH * c, SH))
        for d in range(1, C):
            go(remote(shard, mine, ra_send.at[v, d], ra_recv.at[v, c], r, other(d)))
        mine[...] = shard[...]

    def wait_rows(v):
        for d in range(1, C):
            landed(row(v, at(SH * other(d), SH)), ra_send.at[v, d], ra_recv.at[v, other(d)])

    def piece(v, block, i):
        aligned = lax.rem(block, 2) == half
        source = jnp.where(aligned, block, lax.rem(block + Z - 1, Z))
        sender = lax.rem(c + jnp.where(aligned, 4, 0) + i, C)
        return column(v, at(((sender // 2) * 4 + source // 2) * NB + lax.rem(sender, 2) * SH, SH))

    def pieces(s, up_way):
        if s < 4:
            return range(4)
        return range(0, 2) if up_way else range(2, 4)

    def ring_copy(v, s, i, up_way, block):
        k = 0 if up_way else 1
        to = z_up if up_way else z_down
        ref = piece(v, block, i)
        return remote(ref, ref, rp_send.at[v, k, s - 1, i], rp_recv.at[v, k, s - 1, i], to * X + x, c)

    def ring_wait_piece(v, s, i, up_way):
        if s == 0:
            landed(piece(v, z, i), sp_send.at[v, 0], sp_recv.at[v, i])
            return
        block = lax.rem(z - s + Z, Z) if up_way else lax.rem(z + s, Z)
        ring_copy(v, s, i, up_way, block).wait_recv()

    def ring(v, s):
        for i in range(4):
            if s == 1:
                ring_wait_piece(v, 0, i, True)
            for up_way in (True, False):
                if i not in pieces(s, up_way):
                    continue
                if s > 1:
                    ring_wait_piece(v, s - 1, i, up_way)
                block = lax.rem(z - (s - 1) + Z, Z) if up_way else lax.rem(z + s - 1, Z)
                go(ring_copy(v, s, i, up_way, block))

    def ring_end(v):
        for up_way in (True, False):
            for i in range(4):
                if i not in pieces(4, up_way):
                    ring_wait_piece(v, 3, i, up_way)
            for i in pieces(4, up_way):
                ring_wait_piece(v, 4, i, up_way)

    def reduce_start(q):
        for d in range(1, C):
            go(remote(part.at[q, at(SH * other(d), SH)], rsb.at[q, d - 1], rs_send.at[q, d], rs_recv.at[q, d], r, other(d)))

    def reduce_end(q):
        total = part[q, at(SH * c, SH), :]
        for d in range(1, C):
            landed(rsb.at[q, d - 1], rs_send.at[q, d], rs_recv.at[q, d])
            total = total + rsb[q, d - 1]
        ysh[q] = total

    sizes = (2 * NB, 2 * NB, 3 * NB, NB)

    def sum_start(e):
        m = sizes[e] // C
        xb[e, x, 0:m, :] = pstack[e, at(m * c, m), :]
        for d in range(1, X):
            go(remote(
                pstack.at[e, at(m * c, m)], xb.at[e, x, 0:m], px_send.at[e, d], px_recv.at[e, x],
                z * X + lax.rem(x + d, X), c,
            ))

    def sum_z(e):
        m = sizes[e] // C
        for d in range(1, X):
            k = lax.rem(x + d, X)
            landed(xb.at[e, k, 0:m], px_send.at[e, d], px_recv.at[e, k])
        zb[e, z, 0:m, :] = (xb[e, 0, 0:m, :] + xb[e, 1, 0:m, :]) + (xb[e, 2, 0:m, :] + xb[e, 3, 0:m, :])
        for d in range(1, Z):
            ref = zb.at[e, z, 0:m]
            go(remote(ref, ref, pz_send.at[e, d], pz_recv.at[e, z], lax.rem(z + d, Z) * X + x, c))

    def sum_col(e):
        m = sizes[e] // C
        for d in range(1, Z):
            k = lax.rem(z + d, Z)
            landed(zb.at[e, k, 0:m], pz_send.at[e, d], pz_recv.at[e, k])
        total = zb[e, 0, 0:m, :]
        for k in range(1, Z):
            total = total + zb[e, k, 0:m, :]
        gsum[e, at(m * c, m), :] = total
        for d in range(1, C):
            ref = gsum.at[e, at(m * c, m)]
            go(remote(ref, ref, pc_send.at[e, d], pc_recv.at[e, c], r, other(d)))

    def sum_end(e):
        m = sizes[e] // C
        for d in range(1, C):
            landed(gsum.at[e, at(m * other(d), m)], pc_send.at[e, d], pc_recv.at[e, other(d)])

    inner = ((1,), (0,))
    both_last = ((1,), (1,))

    def fold(value):
        return value[:, 0:NB] + value[:, NB : 2 * NB]

    def split_h():
        @pl.loop(0, 8)
        def _(j):
            rows = pl.ds(pl.multiple_of(j * SH, SH), SH)
            hh[rows, :], hl[rows, :] = halves(hv[rows, :])

    def times_h(q):
        @pl.loop(0, 2)
        def _(j):
            rows = pl.ds(pl.multiple_of(j * 2 * NB, 2 * NB), 2 * NB)
            part[q, rows, :] = fold(dot_b(hh[rows, :], vs[...], inner) + dot_b(hl[rows, :], vs[...], inner))

    eye = lax.broadcasted_iota(jnp.int32, (NB, NB), 0) == lax.broadcasted_iota(jnp.int32, (NB, NB), 1)

    def scaled(q, e):
        gram = gsum[e, 0:NB, :]
        diagonal = jnp.where(eye, gram, 0.0)
        sc1[q] = jnp.broadcast_to(lax.rsqrt(jnp.sum(diagonal, axis=0, keepdims=True)), (NB, NB))
        sc2[q] = jnp.broadcast_to(lax.rsqrt(jnp.sum(diagonal, axis=1, keepdims=True)), (NB, NB))
        inv[q] = gram * sc1[q] * sc2[q]

    def sweep(q, groups):
        inv[q] = sweep_steps(inv[q], groups)

    def factors(p, y, k, s, d):
        pk = dot(p * d[0:1, :], k)
        alpha = -2.0 * pk * d[0:1, :]
        beta = dot(4.0 * dot(pk, s) - 2.0 * (y * d[0:1, :]), k) * d[0:1, :]
        return alpha, beta

    finish_p = scatter(PV)
    finish_c = scatter(CV)
    finish_p()

    @pl.when((r == 0) & (c < 2))
    def _():
        sh[PV] = jnp.zeros((SH, NB), F32)

    distribute(PV, sh.at[PV])
    ring(PV, 1)
    wait_rows(PV)
    p1 = ypr[:, NB : 2 * NB]
    pstack[0, 0:NB, :] = dot_tn(p1, p1)
    pstack[0, NB : 2 * NB, :] = jnp.where(r == 1, ypr[0:NB, NB : 2 * NB], 0.0)
    sum_start(0)
    ring(PV, 2)
    sum_z(0)
    ring(PV, 3)
    finish_c()
    distribute(CV, sh.at[CV])
    copy_h.wait()
    split_h()
    ring(PV, 4)
    sum_col(0)
    ring_end(PV)

    @pl.loop(0, 8)
    def _(k):
        rows = pl.ds(pl.multiple_of(k * 2 * NB, 2 * NB), 2 * NB)
        vs[rows, 0:NB], vs[rows, NB : 2 * NB] = halves(yp[rows, NB : 2 * NB])

    times_h(0)
    reduce_start(0)
    sum_end(0)
    scaled(0, 0)
    ring(CV, 1)
    sweep(0, 4)
    reduce_end(0)
    distribute(YV, ysh.at[0])
    ring(CV, 2)
    sweep(0, 6)
    ring(YV, 1)
    ring(CV, 3)
    wait_rows(CV)
    wait_rows(YV)
    pstack[1, 0:NB, :] = dot_tn(ypr[:, NB : 2 * NB], ypr[:, 0:NB])
    pstack[1, NB : 2 * NB, :] = dot_tn(cr[...], ypr[:, NB : 2 * NB])
    sum_start(1)
    sweep(0, 6)
    ring(YV, 2)
    ring(CV, 4)
    sum_z(1)
    ring(YV, 3)
    sum_col(1)
    ring(YV, 4)
    sum_end(1)
    k1, d1, e1 = inv[0], sc1[0], sc2[0]
    s1 = gsum[1, 0:NB, :] * d1 * e1
    alpha_b, beta_b = factors(gsum[0, NB : 2 * NB, :], gsum[1, NB : 2 * NB, :], k1, s1, d1)
    abt[0:NB, :] = alpha_b.T
    abt[NB : 2 * NB, :] = beta_b.T
    abts[:, 0:NB], abts[:, NB : 2 * NB] = halves(abt[...])
    p2r[...] = cr[...] + dot(ypr[...], abt[...])

    @pl.when(r < 2)
    def _():
        p2r[0:NB, :] = jnp.zeros((NB, NB), F32)

    pstack[2, 0:NB, :] = dot_tn(p2r[...], p2r[...])
    pstack[2, NB : 3 * NB, :] = dot_tn(ypr[...], p2r[...])
    sum_start(2)
    ring_end(CV)
    ring_end(YV)

    @pl.loop(0, 8)
    def _(k):
        rows = pl.ds(pl.multiple_of(k * 2 * NB, 2 * NB), 2 * NB)
        high, low = halves(yp[rows, :])
        value = cform[rows, :] + fold(dot_b(high, abts[...], inner) + dot_b(low, abts[...], inner))
        sub = lax.broadcasted_iota(jnp.int32, (2 * NB, NB), 0)
        value = jnp.where((sub < NB) & (k == 0) & (c < 2), 0.0, value)
        up[rows, NB : 2 * NB] = value
        vs[rows, 0:NB], vs[rows, NB : 2 * NB] = halves(value)

    sum_z(2)
    times_h(1)
    reduce_start(1)
    sum_col(2)
    alpha1, beta1 = factors(ypr[:, NB : 2 * NB], ypr[:, 0:NB], k1, s1, d1)
    ab1[:, 0:NB] = alpha1
    ab1[:, NB : 2 * NB] = beta1
    reduce_end(1)
    distribute(UV, ysh.at[1])
    sum_end(2)
    scaled(1, 2)
    sweep(1, 4)
    ring(UV, 1)
    wait_rows(UV)
    pstack[3, 0:NB, :] = dot_tn(p2r[...], ur[...])
    sum_start(3)
    sweep(1, 6)
    ring(UV, 2)
    sum_z(3)
    sweep(1, 6)
    ring(UV, 3)
    sum_col(3)
    k2, d2, e2 = inv[1], sc1[1], sc2[1]
    t1, t2 = gsum[2, NB : 2 * NB, :], gsum[2, 2 * NB : 3 * NB, :]
    kt2 = dot(k1, t2 * e1)
    ab[0:NB, :] = -2.0 * kt2 * e1
    ab[NB : 2 * NB, :] = dot(k1, 4.0 * dot(s1, kt2) - 2.0 * (t1 * e1)) * e1
    pk2 = dot(p2r[...] * d2[0:1, :], k2)
    alpha2 = -2.0 * pk2 * d2[0:1, :]
    lhs_ref[0, :, 0:NB], lhs_ref[1, :, 0:NB] = halves(alpha2)
    abh[0], abh[1] = halves(ab1[...] + dot_nt(alpha2, ab[...]))
    y2 = ur[...] + dot(ypr[...], ab[...])
    ring(UV, 4)

    @pl.loop(0, 8)
    def _(k):
        cols = pl.ds(pl.multiple_of(k * 2 * NB, 2 * NB), 2 * NB)
        high, low = halves(yp[cols, :])
        hv[:, cols] = hv[:, cols] + (
            dot_b(abh[0], high, both_last) + (dot_b(abh[0], low, both_last) + dot_b(abh[1], high, both_last))
        )

    sum_end(3)
    s2 = (gsum[3, 0:NB, :] + dot_tn(gsum[2, NB : 3 * NB, :], ab[...])) * d2 * e2
    beta2 = dot(4.0 * dot(pk2, s2) - 2.0 * (y2 * d2[0:1, :]), k2) * d2[0:1, :]
    lhs_ref[0, :, NB : 2 * NB], lhs_ref[1, :, NB : 2 * NB] = halves(beta2)
    ring_end(UV)
    for copy in started:
        copy.wait_send()


def factors_kernel(hamiltonian):
    rows, cols = hamiltonian.shape
    dma = pltpu.SemaphoreType.DMA
    vmem = pl.BlockSpec(memory_space=pltpu.VMEM)
    return pl.pallas_call(
        kernel,
        out_shape=(
            pltpu.VMEM((rows, cols), F32),
            pltpu.VMEM((2, rows, 2 * NB), BF16),
            pltpu.VMEM((cols, 2 * NB), F32),
        ),
        in_specs=[pl.BlockSpec(memory_space=pltpu.HBM)],
        out_specs=(vmem, vmem, vmem),
        scratch_shapes=[
            pltpu.VMEM((2, SH, NB), F32),
            pltpu.VMEM((cols, 2 * NB), F32),
            pltpu.VMEM((cols, NB), F32),
            pltpu.VMEM((rows, 2 * NB), F32),
            pltpu.VMEM((rows, NB), F32),
            pltpu.VMEM((rows, NB), F32),
            pltpu.VMEM((rows, NB), F32),
            pltpu.VMEM((rows, 2 * NB), F32),
            pltpu.VMEM((2, rows, NB), F32),
            pltpu.VMEM((2, C - 1, SH, NB), F32),
            pltpu.VMEM((2, SH, NB), F32),
            pltpu.VMEM((2 * NB, NB), F32),
            pltpu.VMEM((2 * NB, NB), F32),
            pltpu.VMEM((4, 3 * NB, NB), F32),
            pltpu.VMEM((4, X, 3 * NB // C, NB), F32),
            pltpu.VMEM((4, Z, 3 * NB // C, NB), F32),
            pltpu.VMEM((4, 3 * NB, NB), F32),
            pltpu.VMEM((2, NB, NB), F32),
            pltpu.VMEM((2, NB, NB), F32),
            pltpu.VMEM((2, NB, NB), F32),
            pltpu.VMEM((rows, cols), BF16),
            pltpu.VMEM((rows, cols), BF16),
            pltpu.VMEM((cols, 2 * NB), BF16),
            pltpu.VMEM((2 * NB, 2 * NB), BF16),
            pltpu.VMEM((2, rows, 2 * NB), BF16),
            dma, dma((2,)), dma((2, C)), dma((2,)),
            dma((4, C)), dma((4, C)), dma((4, 4)), dma((4, 4)),
            dma((4, 2, 4, 4)), dma((4, 2, 4, 4)),
            dma((2, C)), dma((2, C)),
            dma((4, X)), dma((4, X)), dma((4, Z)), dma((4, Z)), dma((4, C)), dma((4, C)),
        ],
        compiler_params=pltpu.CompilerParams(
            collective_id=0, has_side_effects=True, vmem_limit_bytes=36 * 1024 * 1024
        ),
        name="reflector_factors",
    )(hamiltonian)


def update_kernel(h_ref, lhs_ref, up_ref, out_ref):
    cols = pl.ds(pl.multiple_of(pl.program_id(0) * 2 * NB, 2 * NB), 2 * NB)
    high, low = halves(up_ref[cols, :])
    last = ((1,), (1,))
    out_ref[...] = h_ref[:, cols] + (
        dot_b(lhs_ref[0], high, last) + (dot_b(lhs_ref[0], low, last) + dot_b(lhs_ref[1], high, last))
    )


def update(partly, lhs, up):
    rows, cols = partly.shape
    vmem = pl.BlockSpec(memory_space=pltpu.VMEM)
    return pl.pallas_call(
        update_kernel,
        grid=(cols // (2 * NB),),
        out_shape=jax.ShapeDtypeStruct((rows, cols), F32),
        in_specs=[vmem, vmem, vmem],
        out_specs=pl.BlockSpec((rows, 2 * NB), lambda i: (0, i)),
        compiler_params=pltpu.CompilerParams(vmem_limit_bytes=20 * 1024 * 1024),
        name="apply_factors",
    )(partly, lhs, up)


def body(hamiltonian):
    return update(*factors_kernel(pltpu.with_memory_space_constraint(hamiltonian, pltpu.HBM)))


def solution(mesh):
    return jax.shard_map(
        body, mesh=mesh, in_specs=(P("row", "col"),), out_specs=P("row", "col"), check_vma=False
    )
```

```python
import functools

import jax
import jax.numpy as jnp
from jax import lax
from jax.experimental import pallas as pl
from jax.experimental.pallas import tpu as pltpu
from jax.sharding import PartitionSpec as P

NB = 128
Z, X, C = 8, 4, 8
SH = 64
HS = 32
MESH = pl.DeviceIdType.MESH
HIGH = lax.Precision.HIGHEST
F32 = jnp.float32
BF16 = jnp.bfloat16


def dot(a, b):
    return lax.dot_general(a, b, (((1,), (0,)), ((), ())), precision=HIGH, preferred_element_type=F32)


def dot_nt(a, b):
    return lax.dot_general(a, b, (((1,), (1,)), ((), ())), precision=HIGH, preferred_element_type=F32)


def dot_tn(a, b):
    return lax.dot_general(a, b, (((0,), (0,)), ((), ())), precision=HIGH, preferred_element_type=F32)


def dot_b(a, b, contract):
    return lax.dot_general(a, b, (contract, ((), ())), preferred_element_type=F32)


def halves(value):
    high = value.astype(BF16)
    return high, (value - high.astype(F32)).astype(BF16)


def invert4(m):
    f = 1.0 / (m[0, 0] * m[1, 1] - m[0, 1] * m[0, 1])
    a00, a01, a11 = m[1, 1] * f, -m[0, 1] * f, m[0, 0] * f
    t00, t01 = a00 * m[0, 2] + a01 * m[1, 2], a00 * m[0, 3] + a01 * m[1, 3]
    t10, t11 = a01 * m[0, 2] + a11 * m[1, 2], a01 * m[0, 3] + a11 * m[1, 3]
    s00 = m[2, 2] - (m[0, 2] * t00 + m[1, 2] * t10)
    s01 = m[2, 3] - (m[0, 2] * t01 + m[1, 2] * t11)
    s11 = m[3, 3] - (m[0, 3] * t01 + m[1, 3] * t11)
    g = 1.0 / (s00 * s11 - s01 * s01)
    u00, u01, u11 = s11 * g, -s01 * g, s00 * g
    w00, w01 = -(t00 * u00 + t01 * u01), -(t00 * u01 + t01 * u11)
    w10, w11 = -(t10 * u00 + t11 * u01), -(t10 * u01 + t11 * u11)
    x00 = a00 - (w00 * t00 + w01 * t01)
    x01 = a01 - (w00 * t10 + w01 * t11)
    x11 = a11 - (w10 * t10 + w11 * t11)
    return ((x00, x01, w00, w01), (x01, x11, w10, w11), (w00, w10, u00, u01), (w01, w11, u01, u11))


def sweep_steps(a, groups):
    tile = (8, NB)
    lane = lax.broadcasted_iota(jnp.int32, tile, 1)
    sub = lax.broadcasted_iota(jnp.int32, tile, 0)

    def group(_, a):
        for t in (0, 4):
            rows = [jnp.broadcast_to(a[0, t + i : t + i + 1, :], tile) for i in range(4)]
            block = {
                (i, j): jnp.broadcast_to(rows[i][:, t + j : t + j + 1], tile) for i in range(4) for j in range(i, 4)
            }
            inverse = invert4(block)
            pivot_lane = (lane >= t) & (lane < t + 4)
            rest = jnp.where(pivot_lane[None], 0.0, a)
            new = []
            for i in range(4):
                v = inverse[i]
                n = (v[0] * rows[0] + v[1] * rows[1]) + (v[2] * rows[2] + v[3] * rows[3])
                for j in range(4):
                    n = jnp.where(lane == t + j, v[j], n)
                new.append(n)
                rest = rest - jnp.broadcast_to(a[:, :, t + i : t + i + 1], a.shape) * n[None]
            top = rest[0]
            for i in range(4):
                top = jnp.where(sub == t + i, new[i], top)
            a = jnp.concatenate([top[None], rest[1:]], axis=0)
        a = jnp.concatenate([a[1:], a[:1]], axis=0)
        return pltpu.roll(a, NB - 8, 2)

    return lax.fori_loop(0, groups, group, a.reshape(NB // 8, 8, NB)).reshape(NB, NB)


def kernel(
    h_hbm, hv, lhs_ref, up,
    sh, yp, cform, ypr, cr, ur, p2r, ab1, part, rsb, ysh, abt, ab,
    pstack, xb, zb, gsum, inv, sc1, sc2, hh, hl, vs, abts, abh,
    h_sem, loc_sem, sc_send, sc_recv, v_send, ra_recv, sp_recv, rp_recv, rx_recv,
    rs_send, rs_recv, p_send, px_recv, pz_recv, pc_recv,
):
    r = lax.axis_index("row")
    c = lax.axis_index("col")
    z = r // X
    x = lax.rem(r, X)
    plane = lax.rem(r, C)
    rel = lax.rem(c - plane + C, C)
    z_up = lax.rem(z + 1, Z)
    z_down = lax.rem(z + Z - 1, Z)
    z_to = jnp.where(rel < 4, z_up, z)
    half = c // 4
    same = lax.rem(z, 2) == half
    z_from = jnp.where(same, z, z_down)

    def remote(src, dst, send, recv, row, col):
        return pltpu.make_async_remote_copy(
            src_ref=src, dst_ref=dst, send_sem=send, recv_sem=recv,
            device_id=(row, col), device_id_type=MESH,
        )

    def landed(rows, sem):
        ref = cform.at[pl.ds(0, rows)]
        remote(ref, ref, sem, sem, r, c).wait_recv()

    def other(d):
        return lax.rem(c + d, C)

    def go(copy):
        copy.start()

    copy_h = pltpu.make_async_copy(h_hbm, hv, h_sem)
    copy_h.start()

    barrier = pltpu.get_barrier_semaphore()

    def greet(row, col):
        pl.semaphore_signal(barrier, inc=1, device_id=(row, col), device_id_type=MESH)

    for d in range(1, C):
        greet(r, other(d))
    for i in range(4):
        greet(z_to * X + i, plane)
        greet(z_from * X + lax.rem(c, X), lax.rem(c + jnp.where(same, 4, 0) + i, C))
    for d in range(1, X):
        greet(z * X + lax.rem(x + d, X), c)
    for d in range(1, Z):
        greet(lax.rem(z + d, Z) * X + x, c)
    pl.semaphore_wait(barrier, 25)

    PV, CV, YV, UV = 0, 1, 2, 3

    def column(v, rows):
        if v == CV:
            return cform.at[rows]
        if v == PV:
            return yp.at[rows, NB : 2 * NB]
        return (up if v == UV else yp).at[rows, 0:NB]

    def row(v, rows):
        if v == PV:
            return ypr.at[rows, NB : 2 * NB]
        if v == YV:
            return ypr.at[rows, 0:NB]
        return (cr if v == CV else ur).at[rows]

    def at(start, size):
        return pl.ds(pl.multiple_of(start, 8), size)

    def scatter(v):
        def from_root(d):
            return remote(h_hbm.at[at(SH * other(d), SH), 0:NB], sh.at[v], sc_send.at[v], sc_recv.at[v], r, other(d))

        def own():
            return pltpu.make_async_copy(h_hbm.at[at(SH * c, SH), 0:NB], sh.at[v], loc_sem.at[v])

        @pl.when(c == v)
        def _():
            own().start()
            for d in range(1, C):
                from_root(d).start()

        def finish():
            @pl.when(c == v)
            def _():
                own().wait()
                ref = cform.at[pl.ds(0, (C - 1) * SH)]
                remote(ref, ref, sc_send.at[v], sc_recv.at[v], r, c).wait_send()

            @pl.when(c != v)
            def _():
                from_root(1).wait_recv()

        return finish

    my_off = ((c // 2) * 4 + r // C) * NB + lax.rem(c, 2) * SH

    def distribute(v, shard):
        for i in range(X):
            to = lax.rem(x + i, X)
            part_of = HS * lax.rem(to, 2)
            go(remote(
                shard.at[at(part_of, HS)], column(v, at(my_off + part_of, HS)),
                v_send.at[v], sp_recv.at[v, lax.rem(rel, 4) // 2], z_to * X + to, plane,
            ))
        mine = row(v, at(SH * c, SH))
        for d in range(1, C):
            go(remote(shard, mine, v_send.at[v], ra_recv.at[v], r, other(d)))
        mine[...] = shard[...]

    def wait_rows(v):
        landed((C - 1) * SH, ra_recv.at[v])

    def piece(v, block, i):
        aligned = lax.rem(block, 2) == half
        source = jnp.where(aligned, block, lax.rem(block + Z - 1, Z))
        sender = lax.rem(c + jnp.where(aligned, 4, 0) + i, C)
        off = ((sender // 2) * 4 + source // 2) * NB + lax.rem(sender, 2) * SH + HS * lax.rem(x, 2)
        return column(v, at(off, HS))

    def pass_z(v, s, i, up_way, block):
        k = 0 if up_way else 1
        to = z_up if up_way else z_down
        ref = piece(v, block, i)
        go(remote(ref, ref, v_send.at[v], rp_recv.at[v, k, s - 1, i // 2], to * X + x, c))

    def pass_x(v, i, block):
        to = lax.rem(x + (1 if i < 2 else X - 1), X)
        ref = piece(v, block, i)
        go(remote(ref, ref, v_send.at[v], rx_recv.at[v], z * X + to, c))

    def behind(s, up_way):
        return lax.rem(z - s + Z, Z) if up_way else lax.rem(z + s, Z)

    def ring(v, s):
        for g in (0, 1):
            pair = (2 * g, 2 * g + 1)
            if s == 1:
                landed(2 * HS, sp_recv.at[v, g])
                for i in pair:
                    pass_z(v, 1, i, True, z)
                    pass_z(v, 1, i, False, z)
                for i in pair:
                    pass_x(v, i, z)
                continue
            for up_way in (True, False):
                landed(2 * HS, rp_recv.at[v, 0 if up_way else 1, s - 2, g])
                if s < 4 or up_way == (g == 0):
                    for i in pair:
                        pass_z(v, s, i, up_way, behind(s - 1, up_way))
                for i in pair:
                    pass_x(v, i, behind(s - 1, up_way))

    def ring_last(v):
        for up_way in (True, False):
            g = 0 if up_way else 1
            landed(2 * HS, rp_recv.at[v, g, 3, g])
            for i in (2 * g, 2 * g + 1):
                pass_x(v, i, behind(4, up_way))

    def ring_done(v):
        landed(32 * HS, rx_recv.at[v])

    def reduce_start(q):
        for d in range(1, C):
            go(remote(part.at[q, at(SH * other(d), SH)], rsb.at[q, d - 1], rs_send.at[q], rs_recv.at[q], r, other(d)))

    def reduce_end(q):
        total = part[q, at(SH * c, SH), :]
        landed((C - 1) * SH, rs_recv.at[q])
        for d in range(1, C):
            total = total + rsb[q, d - 1]
        ysh[q] = total

    sizes = (2 * NB, 2 * NB, NB, NB, 2 * NB)

    def sum_start(e):
        m = sizes[e] // C
        xb[e, x, 0:m, :] = pstack[e, at(m * c, m), :]
        for d in range(1, X):
            go(remote(
                pstack.at[e, at(m * c, m)], xb.at[e, x, 0:m], p_send.at[e], px_recv.at[e],
                z * X + lax.rem(x + d, X), c,
            ))

    def sum_z(e):
        m = sizes[e] // C
        landed((X - 1) * m, px_recv.at[e])
        zb[e, z, 0:m, :] = (xb[e, 0, 0:m, :] + xb[e, 1, 0:m, :]) + (xb[e, 2, 0:m, :] + xb[e, 3, 0:m, :])
        for d in range(1, Z):
            ref = zb.at[e, z, 0:m]
            go(remote(ref, ref, p_send.at[e], pz_recv.at[e], lax.rem(z + d, Z) * X + x, c))

    def sum_col(e):
        m = sizes[e] // C
        landed((Z - 1) * m, pz_recv.at[e])
        total = zb[e, 0, 0:m, :]
        for k in range(1, Z):
            total = total + zb[e, k, 0:m, :]
        gsum[e, at(m * c, m), :] = total
        for d in range(1, C):
            ref = gsum.at[e, at(m * c, m)]
            go(remote(ref, ref, p_send.at[e], pc_recv.at[e], r, other(d)))

    def sum_end(e):
        landed((C - 1) * sizes[e] // C, pc_recv.at[e])

    def drain():
        def sent(ref, sem):
            remote(ref, ref, sem, sem, r, c).wait_send()

        for v in range(4):
            sent(yp.at[pl.ds(0, (64 * HS + (C - 1) * SH) // 2)], v_send.at[v])
        for q in range(2):
            sent(cform.at[pl.ds(0, (C - 1) * SH)], rs_send.at[q])
        for e in range(5):
            sent(cform.at[pl.ds(0, (X + Z + C - 3) * sizes[e] // C)], p_send.at[e])

    inner = ((1,), (0,))
    both_last = ((1,), (1,))

    def fold(value):
        return value[:, 0:NB] + value[:, NB : 2 * NB]

    def split_h():
        @pl.loop(0, 8)
        def _(j):
            rows = pl.ds(pl.multiple_of(j * SH, SH), SH)
            hh[rows, :], hl[rows, :] = halves(hv[rows, :])

    def times_h(q):
        @pl.loop(0, 2)
        def _(j):
            rows = pl.ds(pl.multiple_of(j * 2 * NB, 2 * NB), 2 * NB)
            part[q, rows, :] = fold(dot_b(hh[rows, :], vs[...], inner) + dot_b(hl[rows, :], vs[...], inner))

    eye = lax.broadcasted_iota(jnp.int32, (NB, NB), 0) == lax.broadcasted_iota(jnp.int32, (NB, NB), 1)

    def scaled(q, e):
        gram = gsum[e, 0:NB, :]
        diagonal = jnp.where(eye, gram, 0.0)
        sc1[q] = jnp.broadcast_to(lax.rsqrt(jnp.sum(diagonal, axis=0, keepdims=True)), (NB, NB))
        sc2[q] = jnp.broadcast_to(lax.rsqrt(jnp.sum(diagonal, axis=1, keepdims=True)), (NB, NB))
        inv[q] = gram * sc1[q] * sc2[q]

    def sweep(q, groups):
        inv[q] = sweep_steps(inv[q], groups)

    def factors(p, y, k, s, d):
        pk = dot(p * d[0:1, :], k)
        alpha = -2.0 * pk * d[0:1, :]
        beta = dot(4.0 * dot(pk, s) - 2.0 * (y * d[0:1, :]), k) * d[0:1, :]
        return alpha, beta

    finish_p = scatter(PV)
    finish_c = scatter(CV)
    finish_p()

    @pl.when((r == 0) & (c < 2))
    def _():
        sh[PV] = jnp.zeros((SH, NB), F32)

    distribute(PV, sh.at[PV])
    ring(PV, 1)
    wait_rows(PV)
    p1 = ypr[:, NB : 2 * NB]
    pstack[0, 0:NB, :] = dot_tn(p1, p1)
    pstack[0, NB : 2 * NB, :] = jnp.where(r == 1, ypr[0:NB, NB : 2 * NB], 0.0)
    sum_start(0)
    ring(PV, 2)
    sum_z(0)
    ring(PV, 3)
    finish_c()
    distribute(CV, sh.at[CV])
    copy_h.wait()
    split_h()
    ring(PV, 4)
    sum_col(0)
    ring_last(PV)
    ring_done(PV)

    @pl.loop(0, 8)
    def _(k):
        rows = pl.ds(pl.multiple_of(k * 2 * NB, 2 * NB), 2 * NB)
        vs[rows, 0:NB], vs[rows, NB : 2 * NB] = halves(yp[rows, NB : 2 * NB])

    times_h(0)
    reduce_start(0)
    sum_end(0)
    scaled(0, 0)
    ring(CV, 1)
    sweep(0, 6)
    reduce_end(0)
    distribute(YV, ysh.at[0])
    ring(CV, 2)
    sweep(0, 6)
    ring(YV, 1)
    ring(CV, 3)
    wait_rows(CV)
    wait_rows(YV)
    pstack[1, 0:NB, :] = dot_tn(ypr[:, NB : 2 * NB], ypr[:, 0:NB])
    pstack[1, NB : 2 * NB, :] = dot_tn(cr[...], ypr[:, NB : 2 * NB])
    sum_start(1)
    sweep(0, 4)
    ring(YV, 2)
    ring(CV, 4)
    sum_z(1)
    ring(YV, 3)
    ring_last(CV)
    sum_col(1)
    ring(YV, 4)
    sum_end(1)
    k1, d1, e1 = inv[0], sc1[0], sc2[0]
    s1 = gsum[1, 0:NB, :] * d1 * e1
    alpha_b, beta_b = factors(gsum[0, NB : 2 * NB, :], gsum[1, NB : 2 * NB, :], k1, s1, d1)
    abt[0:NB, :] = alpha_b.T
    abt[NB : 2 * NB, :] = beta_b.T
    abts[:, 0:NB], abts[:, NB : 2 * NB] = halves(abt[...])
    p2r[...] = cr[...] + dot(ypr[...], abt[...])

    @pl.when(r < 2)
    def _():
        p2r[0:NB, :] = jnp.zeros((NB, NB), F32)

    pstack[2, 0:NB, :] = dot_tn(p2r[...], p2r[...])
    sum_start(2)
    ring_last(YV)
    ring_done(CV)
    ring_done(YV)

    @pl.loop(0, 8)
    def _(k):
        rows = pl.ds(pl.multiple_of(k * 2 * NB, 2 * NB), 2 * NB)
        high, low = halves(yp[rows, :])
        value = cform[rows, :] + fold(dot_b(high, abts[...], inner) + dot_b(low, abts[...], inner))
        sub = lax.broadcasted_iota(jnp.int32, (2 * NB, NB), 0)
        value = jnp.where((sub < NB) & (k == 0) & (c < 2), 0.0, value)
        up[rows, NB : 2 * NB] = value
        vs[rows, 0:NB], vs[rows, NB : 2 * NB] = halves(value)

    sum_z(2)
    times_h(1)
    reduce_start(1)
    pstack[4] = dot_tn(ypr[...], p2r[...])
    sum_start(4)
    sum_col(2)
    alpha1, beta1 = factors(ypr[:, NB : 2 * NB], ypr[:, 0:NB], k1, s1, d1)
    ab1[:, 0:NB] = alpha1
    ab1[:, NB : 2 * NB] = beta1
    reduce_end(1)
    distribute(UV, ysh.at[1])
    sum_end(2)
    scaled(1, 2)
    sweep(1, 6)
    ring(UV, 1)
    wait_rows(UV)
    pstack[3, 0:NB, :] = dot_tn(p2r[...], ur[...])
    sum_start(3)
    sum_z(4)
    sweep(1, 5)
    ring(UV, 2)
    sum_z(3)
    sweep(1, 5)
    sum_col(4)
    ring(UV, 3)
    sum_col(3)
    k2, d2, e2 = inv[1], sc1[1], sc2[1]
    pk2 = dot(p2r[...] * d2[0:1, :], k2)
    alpha2 = -2.0 * pk2 * d2[0:1, :]
    lhs_ref[0, :, 0:NB], lhs_ref[1, :, 0:NB] = halves(alpha2)
    ring(UV, 4)
    sum_end(4)
    t1, t2 = gsum[4, 0:NB, :], gsum[4, NB : 2 * NB, :]
    kt2 = dot(k1, t2 * e1)
    ab[0:NB, :] = -2.0 * kt2 * e1
    ab[NB : 2 * NB, :] = dot(k1, 4.0 * dot(s1, kt2) - 2.0 * (t1 * e1)) * e1
    abh[0], abh[1] = halves(ab1[...] + dot_nt(alpha2, ab[...]))
    y2 = ur[...] + dot(ypr[...], ab[...])
    ring_last(UV)

    @pl.loop(0, 8)
    def _(k):
        cols = pl.ds(pl.multiple_of(k * 2 * NB, 2 * NB), 2 * NB)
        high, low = halves(yp[cols, :])
        hv[:, cols] = hv[:, cols] + (
            dot_b(abh[0], high, both_last) + (dot_b(abh[0], low, both_last) + dot_b(abh[1], high, both_last))
        )

    sum_end(3)
    s2 = (gsum[3, 0:NB, :] + dot_tn(gsum[4], ab[...])) * d2 * e2
    beta2 = dot(4.0 * dot(pk2, s2) - 2.0 * (y2 * d2[0:1, :]), k2) * d2[0:1, :]
    lhs_ref[0, :, NB : 2 * NB], lhs_ref[1, :, NB : 2 * NB] = halves(beta2)
    ring_done(UV)
    drain()


def factors_kernel(hamiltonian):
    rows, cols = hamiltonian.shape
    dma = pltpu.SemaphoreType.DMA
    vmem = pl.BlockSpec(memory_space=pltpu.VMEM)
    return pl.pallas_call(
        kernel,
        out_shape=(
            pltpu.VMEM((rows, cols), F32),
            pltpu.VMEM((2, rows, 2 * NB), BF16),
            pltpu.VMEM((cols, 2 * NB), F32),
        ),
        in_specs=[pl.BlockSpec(memory_space=pltpu.HBM)],
        out_specs=(vmem, vmem, vmem),
        scratch_shapes=[
            pltpu.VMEM((2, SH, NB), F32),
            pltpu.VMEM((cols, 2 * NB), F32),
            pltpu.VMEM((cols, NB), F32),
            pltpu.VMEM((rows, 2 * NB), F32),
            pltpu.VMEM((rows, NB), F32),
            pltpu.VMEM((rows, NB), F32),
            pltpu.VMEM((rows, NB), F32),
            pltpu.VMEM((rows, 2 * NB), F32),
            pltpu.VMEM((2, rows, NB), F32),
            pltpu.VMEM((2, C - 1, SH, NB), F32),
            pltpu.VMEM((2, SH, NB), F32),
            pltpu.VMEM((2 * NB, NB), F32),
            pltpu.VMEM((2 * NB, NB), F32),
            pltpu.VMEM((5, 2 * NB, NB), F32),
            pltpu.VMEM((5, X, 2 * NB // C, NB), F32),
            pltpu.VMEM((5, Z, 2 * NB // C, NB), F32),
            pltpu.VMEM((5, 2 * NB, NB), F32),
            pltpu.VMEM((2, NB, NB), F32),
            pltpu.VMEM((2, NB, NB), F32),
            pltpu.VMEM((2, NB, NB), F32),
            pltpu.VMEM((rows, cols), BF16),
            pltpu.VMEM((rows, cols), BF16),
            pltpu.VMEM((cols, 2 * NB), BF16),
            pltpu.VMEM((2 * NB, 2 * NB), BF16),
            pltpu.VMEM((2, rows, 2 * NB), BF16),
            dma, dma((2,)), dma((2,)), dma((2,)), dma((4,)), dma((4,)), dma((4, 2)), dma((4, 2, 4, 2)), dma((4,)),
            dma((2,)), dma((2,)), dma((5,)), dma((5,)), dma((5,)), dma((5,)),
        ],
        compiler_params=pltpu.CompilerParams(
            collective_id=0, has_side_effects=True, vmem_limit_bytes=36 * 1024 * 1024
        ),
        name="reflector_factors",
    )(hamiltonian)


def update_kernel(h_ref, lhs_ref, up_ref, out_ref):
    cols = pl.ds(pl.multiple_of(pl.program_id(0) * 2 * NB, 2 * NB), 2 * NB)
    high, low = halves(up_ref[cols, :])
    last = ((1,), (1,))
    out_ref[...] = h_ref[:, cols] + (
        dot_b(lhs_ref[0], high, last) + (dot_b(lhs_ref[0], low, last) + dot_b(lhs_ref[1], high, last))
    )


def update(partly, lhs, up):
    rows, cols = partly.shape
    vmem = pl.BlockSpec(memory_space=pltpu.VMEM)
    return pl.pallas_call(
        update_kernel,
        grid=(cols // (2 * NB),),
        out_shape=jax.ShapeDtypeStruct((rows, cols), F32),
        in_specs=[vmem, vmem, vmem],
        out_specs=pl.BlockSpec((rows, 2 * NB), lambda i: (0, i)),
        compiler_params=pltpu.CompilerParams(vmem_limit_bytes=20 * 1024 * 1024),
        name="apply_factors",
    )(partly, lhs, up)


def body(hamiltonian):
    return update(*factors_kernel(pltpu.with_memory_space_constraint(hamiltonian, pltpu.HBM)))


def solution(mesh):
    return jax.shard_map(
        body, mesh=mesh, in_specs=(P("row", "col"),), out_specs=P("row", "col"), check_vma=False
    )
```

```python
import functools

import jax
import jax.numpy as jnp
from jax import lax
from jax.experimental import pallas as pl
from jax.experimental.pallas import tpu as pltpu
from jax.sharding import PartitionSpec as P

NB = 128
Z, X, C = 8, 4, 8
SH = 64
HS = 32
MESH = pl.DeviceIdType.MESH
HIGH = lax.Precision.HIGHEST
F32 = jnp.float32
BF16 = jnp.bfloat16


def dot(a, b):
    return lax.dot_general(a, b, (((1,), (0,)), ((), ())), precision=HIGH, preferred_element_type=F32)


def dot_nt(a, b):
    return lax.dot_general(a, b, (((1,), (1,)), ((), ())), precision=HIGH, preferred_element_type=F32)


def dot_tn(a, b):
    return lax.dot_general(a, b, (((0,), (0,)), ((), ())), precision=HIGH, preferred_element_type=F32)


def dot_b(a, b, contract):
    return lax.dot_general(a, b, (contract, ((), ())), preferred_element_type=F32)


def halves(value):
    high = value.astype(BF16)
    return high, (value - high.astype(F32)).astype(BF16)


def invert4(m):
    f = 1.0 / (m[0, 0] * m[1, 1] - m[0, 1] * m[0, 1])
    a00, a01, a11 = m[1, 1] * f, -m[0, 1] * f, m[0, 0] * f
    t00, t01 = a00 * m[0, 2] + a01 * m[1, 2], a00 * m[0, 3] + a01 * m[1, 3]
    t10, t11 = a01 * m[0, 2] + a11 * m[1, 2], a01 * m[0, 3] + a11 * m[1, 3]
    s00 = m[2, 2] - (m[0, 2] * t00 + m[1, 2] * t10)
    s01 = m[2, 3] - (m[0, 2] * t01 + m[1, 2] * t11)
    s11 = m[3, 3] - (m[0, 3] * t01 + m[1, 3] * t11)
    g = 1.0 / (s00 * s11 - s01 * s01)
    u00, u01, u11 = s11 * g, -s01 * g, s00 * g
    w00, w01 = -(t00 * u00 + t01 * u01), -(t00 * u01 + t01 * u11)
    w10, w11 = -(t10 * u00 + t11 * u01), -(t10 * u01 + t11 * u11)
    x00 = a00 - (w00 * t00 + w01 * t01)
    x01 = a01 - (w00 * t10 + w01 * t11)
    x11 = a11 - (w10 * t10 + w11 * t11)
    return ((x00, x01, w00, w01), (x01, x11, w10, w11), (w00, w10, u00, u01), (w01, w11, u01, u11))


def sweep_steps(a, groups):
    tile = (8, NB)
    lane = lax.broadcasted_iota(jnp.int32, tile, 1)
    sub = lax.broadcasted_iota(jnp.int32, tile, 0)

    def group(_, a):
        for t in (0, 4):
            rows = [jnp.broadcast_to(a[0, t + i : t + i + 1, :], tile) for i in range(4)]
            block = {
                (i, j): jnp.broadcast_to(rows[i][:, t + j : t + j + 1], tile) for i in range(4) for j in range(i, 4)
            }
            inverse = invert4(block)
            pivot_lane = (lane >= t) & (lane < t + 4)
            rest = jnp.where(pivot_lane[None], 0.0, a)
            new = []
            for i in range(4):
                v = inverse[i]
                n = (v[0] * rows[0] + v[1] * rows[1]) + (v[2] * rows[2] + v[3] * rows[3])
                for j in range(4):
                    n = jnp.where(lane == t + j, v[j], n)
                new.append(n)
                rest = rest - jnp.broadcast_to(a[:, :, t + i : t + i + 1], a.shape) * n[None]
            top = rest[0]
            for i in range(4):
                top = jnp.where(sub == t + i, new[i], top)
            a = jnp.concatenate([top[None], rest[1:]], axis=0)
        a = jnp.concatenate([a[1:], a[:1]], axis=0)
        return pltpu.roll(a, NB - 8, 2)

    return lax.fori_loop(0, groups, group, a.reshape(NB // 8, 8, NB)).reshape(NB, NB)


def kernel(
    h_hbm, hv, lhs_ref, up, rest,
    sh, yp, cform, ypr, cr, ur, p2r, part, rsb, ysh, abt, ab,
    pstack, xb, zb, gsum, inv, sc1, sc2, hh, hl, vs, abts, abh,
    h_sem, loc_sem, sc_send, sc_recv, v_send, ra_recv, sp_recv, rp_recv, rx_recv,
    rs_send, rs_recv, p_send, px_recv, pz_recv, pc_recv,
):
    r = lax.axis_index("row")
    c = lax.axis_index("col")
    z = r // X
    x = lax.rem(r, X)
    plane = lax.rem(r, C)
    rel = lax.rem(c - plane + C, C)
    z_up = lax.rem(z + 1, Z)
    z_down = lax.rem(z + Z - 1, Z)
    z_to = jnp.where(rel < 4, z_up, z)
    half = c // 4
    same = lax.rem(z, 2) == half
    z_from = jnp.where(same, z, z_down)

    def remote(src, dst, send, recv, row, col):
        return pltpu.make_async_remote_copy(
            src_ref=src, dst_ref=dst, send_sem=send, recv_sem=recv,
            device_id=(row, col), device_id_type=MESH,
        )

    def landed(rows, sem):
        ref = cform.at[pl.ds(0, rows)]
        remote(ref, ref, sem, sem, r, c).wait_recv()

    def other(d):
        return lax.rem(c + d, C)

    def go(copy):
        copy.start()

    copy_h = pltpu.make_async_copy(h_hbm, hv, h_sem)
    copy_h.start()

    barrier = pltpu.get_barrier_semaphore()

    def greet(row, col):
        pl.semaphore_signal(barrier, inc=1, device_id=(row, col), device_id_type=MESH)

    for d in range(1, C):
        greet(r, other(d))
    for i in range(4):
        greet(z_to * X + i, plane)
        greet(z_from * X + lax.rem(c, X), lax.rem(c + jnp.where(same, 4, 0) + i, C))
    for d in range(1, X):
        greet(z * X + lax.rem(x + d, X), c)
    for d in range(1, Z):
        greet(lax.rem(z + d, Z) * X + x, c)
    pl.semaphore_wait(barrier, 25)

    PV, CV, YV, UV = 0, 1, 2, 3

    def column(v, rows):
        if v == CV:
            return cform.at[rows]
        if v == PV:
            return yp.at[rows, NB : 2 * NB]
        return (up if v == UV else yp).at[rows, 0:NB]

    def row(v, rows):
        if v == PV:
            return ypr.at[rows, NB : 2 * NB]
        if v == YV:
            return ypr.at[rows, 0:NB]
        return (cr if v == CV else ur).at[rows]

    def at(start, size):
        return pl.ds(pl.multiple_of(start, 8), size)

    def scatter(v):
        def from_root(d):
            return remote(h_hbm.at[at(SH * other(d), SH), 0:NB], sh.at[v], sc_send.at[v], sc_recv.at[v], r, other(d))

        def own():
            return pltpu.make_async_copy(h_hbm.at[at(SH * c, SH), 0:NB], sh.at[v], loc_sem.at[v])

        @pl.when(c == v)
        def _():
            own().start()
            for d in range(1, C):
                from_root(d).start()

        def finish():
            @pl.when(c == v)
            def _():
                own().wait()
                ref = cform.at[pl.ds(0, (C - 1) * SH)]
                remote(ref, ref, sc_send.at[v], sc_recv.at[v], r, c).wait_send()

            @pl.when(c != v)
            def _():
                from_root(1).wait_recv()

        return finish

    my_off = ((c // 2) * 4 + r // C) * NB + lax.rem(c, 2) * SH

    def distribute(v, shard):
        for i in range(X):
            to = lax.rem(x + i, X)
            part_of = HS * lax.rem(to, 2)
            go(remote(
                shard.at[at(part_of, HS)], column(v, at(my_off + part_of, HS)),
                v_send.at[v], sp_recv.at[v, lax.rem(rel, 4) // 2], z_to * X + to, plane,
            ))
        mine = row(v, at(SH * c, SH))
        for d in range(1, C):
            go(remote(shard, mine, v_send.at[v], ra_recv.at[v], r, other(d)))
        mine[...] = shard[...]

    def wait_rows(v):
        landed((C - 1) * SH, ra_recv.at[v])

    def piece(v, block, i):
        aligned = lax.rem(block, 2) == half
        source = jnp.where(aligned, block, lax.rem(block + Z - 1, Z))
        sender = lax.rem(c + jnp.where(aligned, 4, 0) + i, C)
        off = ((sender // 2) * 4 + source // 2) * NB + lax.rem(sender, 2) * SH + HS * lax.rem(x, 2)
        return column(v, at(off, HS))

    def pass_z(v, s, i, up_way, block):
        k = 0 if up_way else 1
        to = z_up if up_way else z_down
        ref = piece(v, block, i)
        go(remote(ref, ref, v_send.at[v], rp_recv.at[v, k, s - 1, i // 2], to * X + x, c))

    def pass_x(v, i, block):
        to = lax.rem(x + (1 if i < 2 else X - 1), X)
        ref = piece(v, block, i)
        go(remote(ref, ref, v_send.at[v], rx_recv.at[v], z * X + to, c))

    def behind(s, up_way):
        return lax.rem(z - s + Z, Z) if up_way else lax.rem(z + s, Z)

    def ring(v, s):
        for g in (0, 1):
            pair = (2 * g, 2 * g + 1)
            if s == 1:
                landed(2 * HS, sp_recv.at[v, g])
                for i in pair:
                    pass_z(v, 1, i, True, z)
                    pass_z(v, 1, i, False, z)
                for i in pair:
                    pass_x(v, i, z)
                continue
            for up_way in (True, False):
                landed(2 * HS, rp_recv.at[v, 0 if up_way else 1, s - 2, g])
                if s < 4 or up_way == (g == 0):
                    for i in pair:
                        pass_z(v, s, i, up_way, behind(s - 1, up_way))
                for i in pair:
                    pass_x(v, i, behind(s - 1, up_way))

    def ring_last(v):
        for up_way in (True, False):
            g = 0 if up_way else 1
            landed(2 * HS, rp_recv.at[v, g, 3, g])
            for i in (2 * g, 2 * g + 1):
                pass_x(v, i, behind(4, up_way))

    def ring_done(v):
        landed(32 * HS, rx_recv.at[v])

    def reduce_start(q):
        for d in range(1, C):
            go(remote(part.at[q, at(SH * other(d), SH)], rsb.at[q, d - 1], rs_send.at[q], rs_recv.at[q], r, other(d)))

    def reduce_end(q):
        total = part[q, at(SH * c, SH), :]
        landed((C - 1) * SH, rs_recv.at[q])
        for d in range(1, C):
            total = total + rsb[q, d - 1]
        ysh[q] = total

    sizes = (NB, NB, NB, NB, 2 * NB, 2 * NB)

    def sum_start(e):
        m = sizes[e] // C
        xb[e, x, 0:m, :] = pstack[e, at(m * c, m), :]
        for d in range(1, X):
            go(remote(
                pstack.at[e, at(m * c, m)], xb.at[e, x, 0:m], p_send.at[e], px_recv.at[e],
                z * X + lax.rem(x + d, X), c,
            ))

    def sum_z(e):
        m = sizes[e] // C
        landed((X - 1) * m, px_recv.at[e])
        zb[e, z, 0:m, :] = (xb[e, 0, 0:m, :] + xb[e, 1, 0:m, :]) + (xb[e, 2, 0:m, :] + xb[e, 3, 0:m, :])
        for d in range(1, Z):
            ref = zb.at[e, z, 0:m]
            go(remote(ref, ref, p_send.at[e], pz_recv.at[e], lax.rem(z + d, Z) * X + x, c))

    def sum_col(e):
        m = sizes[e] // C
        landed((Z - 1) * m, pz_recv.at[e])
        total = zb[e, 0, 0:m, :]
        for k in range(1, Z):
            total = total + zb[e, k, 0:m, :]
        gsum[e, at(m * c, m), :] = total
        for d in range(1, C):
            ref = gsum.at[e, at(m * c, m)]
            go(remote(ref, ref, p_send.at[e], pc_recv.at[e], r, other(d)))

    def sum_end(e):
        landed((C - 1) * sizes[e] // C, pc_recv.at[e])

    def drain():
        def sent(ref, sem):
            remote(ref, ref, sem, sem, r, c).wait_send()

        for v in range(4):
            sent(yp.at[pl.ds(0, (64 * HS + (C - 1) * SH) // 2)], v_send.at[v])
        for q in range(2):
            sent(cform.at[pl.ds(0, (C - 1) * SH)], rs_send.at[q])
        for e in range(6):
            sent(cform.at[pl.ds(0, (X + Z + C - 3) * sizes[e] // C)], p_send.at[e])

    inner = ((1,), (0,))
    both_last = ((1,), (1,))

    def fold(value):
        return value[:, 0:NB] + value[:, NB : 2 * NB]

    def split_h():
        @pl.loop(0, 8)
        def _(j):
            rows = pl.ds(pl.multiple_of(j * SH, SH), SH)
            hh[rows, :], hl[rows, :] = halves(hv[rows, :])

    def times_h(q):
        @pl.loop(0, 2)
        def _(j):
            rows = pl.ds(pl.multiple_of(j * 2 * NB, 2 * NB), 2 * NB)
            part[q, rows, :] = fold(dot_b(hh[rows, :], vs[...], inner) + dot_b(hl[rows, :], vs[...], inner))

    eye = lax.broadcasted_iota(jnp.int32, (NB, NB), 0) == lax.broadcasted_iota(jnp.int32, (NB, NB), 1)

    def scaled(q, e):
        gram = gsum[e, 0:NB, :]
        diagonal = jnp.where(eye, gram, 0.0)
        sc1[q] = jnp.broadcast_to(lax.rsqrt(jnp.sum(diagonal, axis=0, keepdims=True)), (NB, NB))
        sc2[q] = jnp.broadcast_to(lax.rsqrt(jnp.sum(diagonal, axis=1, keepdims=True)), (NB, NB))
        inv[q] = gram * sc1[q] * sc2[q]

    def sweep(q, groups):
        inv[q] = sweep_steps(inv[q], groups)

    def factors(p, y, k, s, d):
        pk = dot(p * d[0:1, :], k)
        alpha = -2.0 * pk * d[0:1, :]
        beta = dot(4.0 * dot(pk, s) - 2.0 * (y * d[0:1, :]), k) * d[0:1, :]
        return alpha, beta

    def apply_panel1(first, last):
        @pl.loop(first, last)
        def _(k):
            cols = pl.ds(pl.multiple_of(k * 2 * NB, 2 * NB), 2 * NB)
            high, low = halves(yp[cols, :])
            hv[:, cols] = hv[:, cols] + (
                dot_b(abh[0], high, both_last) + (dot_b(abh[0], low, both_last) + dot_b(abh[1], high, both_last))
            )

    finish_p = scatter(PV)
    finish_p()

    @pl.when((r == 0) & (c < 2))
    def _():
        sh[PV] = jnp.zeros((SH, NB), F32)

    distribute(PV, sh.at[PV])
    finish_c = scatter(CV)
    ring(PV, 1)
    wait_rows(PV)
    p1 = ypr[:, NB : 2 * NB]
    pstack[0, 0:NB, :] = dot_tn(p1, p1)
    sum_start(0)
    ring(PV, 2)
    sum_z(0)
    ring(PV, 3)
    finish_c()
    distribute(CV, sh.at[CV])
    copy_h.wait()
    split_h()
    ring(PV, 4)
    sum_col(0)
    ring_last(PV)
    ring(CV, 1)
    ring_done(PV)

    @pl.loop(0, 8)
    def _(k):
        rows = pl.ds(pl.multiple_of(k * 2 * NB, 2 * NB), 2 * NB)
        vs[rows, 0:NB], vs[rows, NB : 2 * NB] = halves(yp[rows, NB : 2 * NB])

    times_h(0)
    reduce_start(0)
    ring(CV, 2)
    sum_end(0)
    scaled(0, 0)
    sweep(0, 3)
    ring(CV, 3)
    wait_rows(CV)
    pstack[5, 0:NB, :] = dot_tn(cr[...], ypr[:, NB : 2 * NB])
    pstack[5, NB : 2 * NB, :] = jnp.where(r == 1, ypr[0:NB, NB : 2 * NB], 0.0)
    sum_start(5)
    reduce_end(0)
    distribute(YV, ysh.at[0])
    ring(CV, 4)
    sweep(0, 4)
    sum_z(5)
    ring_last(CV)
    ring(YV, 1)
    wait_rows(YV)
    pstack[1, 0:NB, :] = dot_tn(ypr[:, NB : 2 * NB], ypr[:, 0:NB])
    sum_start(1)
    sweep(0, 3)
    ring(YV, 2)
    sum_z(1)
    sweep(0, 3)
    sum_col(5)
    ring(YV, 3)
    sweep(0, 3)
    sum_col(1)
    ring(YV, 4)
    sum_end(5)
    ring_last(YV)
    sum_end(1)
    k1, d1, e1 = inv[0], sc1[0], sc2[0]
    s1 = gsum[1, 0:NB, :] * d1 * e1
    alpha_b, beta_b = factors(gsum[5, NB : 2 * NB, :], gsum[5, 0:NB, :], k1, s1, d1)
    abt[0:NB, :] = alpha_b.T
    abt[NB : 2 * NB, :] = beta_b.T
    abts[:, 0:NB], abts[:, NB : 2 * NB] = halves(abt[...])
    p2r[...] = cr[...] + dot(ypr[...], abt[...])

    @pl.when(r < 2)
    def _():
        p2r[0:NB, :] = jnp.zeros((NB, NB), F32)

    pstack[2, 0:NB, :] = dot_tn(p2r[...], p2r[...])
    sum_start(2)
    ring_done(CV)
    ring_done(YV)

    @pl.loop(0, 8)
    def _(k):
        rows = pl.ds(pl.multiple_of(k * 2 * NB, 2 * NB), 2 * NB)
        high, low = halves(yp[rows, :])
        value = cform[rows, :] + fold(dot_b(high, abts[...], inner) + dot_b(low, abts[...], inner))
        sub = lax.broadcasted_iota(jnp.int32, (2 * NB, NB), 0)
        value = jnp.where((sub < NB) & (k == 0) & (c < 2), 0.0, value)
        up[rows, NB : 2 * NB] = value
        vs[rows, 0:NB], vs[rows, NB : 2 * NB] = halves(value)

    sum_z(2)
    times_h(1)
    reduce_start(1)
    pstack[4] = dot_tn(ypr[...], p2r[...])
    sum_start(4)
    alpha1, beta1 = factors(ypr[:, NB : 2 * NB], ypr[:, 0:NB], k1, s1, d1)
    abh[0, :, 0:NB], abh[1, :, 0:NB] = halves(alpha1)
    abh[0, :, NB : 2 * NB], abh[1, :, NB : 2 * NB] = halves(beta1)
    sum_col(2)
    apply_panel1(0, 4)
    reduce_end(1)
    distribute(UV, ysh.at[1])
    sum_z(4)
    sum_end(2)
    scaled(1, 2)
    sweep(1, 8)
    ring(UV, 1)
    wait_rows(UV)
    pstack[3, 0:NB, :] = dot_tn(p2r[...], ur[...])
    sum_start(3)
    sweep(1, 3)
    ring(UV, 2)
    sum_z(3)
    sweep(1, 5)
    ring(UV, 3)
    sum_col(4)
    k2, d2, e2 = inv[1], sc1[1], sc2[1]
    pk2 = dot(p2r[...] * d2[0:1, :], k2)
    alpha2 = -2.0 * pk2 * d2[0:1, :]
    lhs_ref[0, :, 0:NB], lhs_ref[1, :, 0:NB] = halves(alpha2)
    apply_panel1(4, 6)
    ring(UV, 4)
    sum_col(3)
    apply_panel1(6, 8)
    sum_end(4)
    t1, t2 = gsum[4, 0:NB, :], gsum[4, NB : 2 * NB, :]
    kt2 = dot(k1, t2 * e1)
    ab[0:NB, :] = -2.0 * kt2 * e1
    ab[NB : 2 * NB, :] = dot(k1, 4.0 * dot(s1, kt2) - 2.0 * (t1 * e1)) * e1
    abts[:, 0:NB], abts[:, NB : 2 * NB] = halves(ab[...])
    ring_last(UV)

    @pl.loop(0, 8)
    def _(k):
        rows = pl.ds(pl.multiple_of(k * 2 * NB, 2 * NB), 2 * NB)
        high, low = halves(yp[rows, :])
        rest[rows, :] = fold(dot_b(high, abts[...], inner) + dot_b(low, abts[...], inner))

    y2 = ur[...] + dot(ypr[...], ab[...])
    sum_end(3)
    s2 = (gsum[3, 0:NB, :] + dot_tn(gsum[4], ab[...])) * d2 * e2
    beta2 = dot(4.0 * dot(pk2, s2) - 2.0 * (y2 * d2[0:1, :]), k2) * d2[0:1, :]
    lhs_ref[0, :, NB : 2 * NB], lhs_ref[1, :, NB : 2 * NB] = halves(beta2)
    ring_done(UV)
    drain()


def factors_kernel(hamiltonian):
    rows, cols = hamiltonian.shape
    dma = pltpu.SemaphoreType.DMA
    vmem = pl.BlockSpec(memory_space=pltpu.VMEM)
    return pl.pallas_call(
        kernel,
        out_shape=(
            pltpu.VMEM((rows, cols), F32),
            pltpu.VMEM((2, rows, 2 * NB), BF16),
            pltpu.VMEM((cols, 2 * NB), F32),
            pltpu.VMEM((cols, NB), F32),
        ),
        in_specs=[pl.BlockSpec(memory_space=pltpu.HBM)],
        out_specs=(vmem, vmem, vmem, vmem),
        scratch_shapes=[
            pltpu.VMEM((2, SH, NB), F32),
            pltpu.VMEM((cols, 2 * NB), F32),
            pltpu.VMEM((cols, NB), F32),
            pltpu.VMEM((rows, 2 * NB), F32),
            pltpu.VMEM((rows, NB), F32),
            pltpu.VMEM((rows, NB), F32),
            pltpu.VMEM((rows, NB), F32),
            pltpu.VMEM((2, rows, NB), F32),
            pltpu.VMEM((2, C - 1, SH, NB), F32),
            pltpu.VMEM((2, SH, NB), F32),
            pltpu.VMEM((2 * NB, NB), F32),
            pltpu.VMEM((2 * NB, NB), F32),
            pltpu.VMEM((6, 2 * NB, NB), F32),
            pltpu.VMEM((6, X, 2 * NB // C, NB), F32),
            pltpu.VMEM((6, Z, 2 * NB // C, NB), F32),
            pltpu.VMEM((6, 2 * NB, NB), F32),
            pltpu.VMEM((2, NB, NB), F32),
            pltpu.VMEM((2, NB, NB), F32),
            pltpu.VMEM((2, NB, NB), F32),
            pltpu.VMEM((rows, cols), BF16),
            pltpu.VMEM((rows, cols), BF16),
            pltpu.VMEM((cols, 2 * NB), BF16),
            pltpu.VMEM((2 * NB, 2 * NB), BF16),
            pltpu.VMEM((2, rows, 2 * NB), BF16),
            dma, dma((2,)), dma((2,)), dma((2,)), dma((4,)), dma((4,)), dma((4, 2)), dma((4, 2, 4, 2)), dma((4,)),
            dma((2,)), dma((2,)), dma((6,)), dma((6,)), dma((6,)), dma((6,)),
        ],
        compiler_params=pltpu.CompilerParams(
            collective_id=0, has_side_effects=True, vmem_limit_bytes=36 * 1024 * 1024
        ),
        name="reflector_factors",
    )(hamiltonian)


def update_kernel(h_ref, lhs_ref, up_ref, rest_ref, out_ref):
    cols = pl.ds(pl.multiple_of(pl.program_id(0) * 2 * NB, 2 * NB), 2 * NB)
    y_high, y_low = halves(up_ref[cols, 0:NB] + rest_ref[cols, :])
    p_high, p_low = halves(up_ref[cols, NB : 2 * NB])
    high = jnp.concatenate([y_high, p_high], axis=1)
    low = jnp.concatenate([y_low, p_low], axis=1)
    last = ((1,), (1,))
    out_ref[...] = h_ref[:, cols] + (
        dot_b(lhs_ref[0], high, last) + (dot_b(lhs_ref[0], low, last) + dot_b(lhs_ref[1], high, last))
    )


def update(partly, lhs, up, rest):
    rows, cols = partly.shape
    vmem = pl.BlockSpec(memory_space=pltpu.VMEM)
    return pl.pallas_call(
        update_kernel,
        grid=(cols // (2 * NB),),
        out_shape=jax.ShapeDtypeStruct((rows, cols), F32),
        in_specs=[vmem, vmem, vmem, vmem],
        out_specs=pl.BlockSpec((rows, 2 * NB), lambda i: (0, i)),
        compiler_params=pltpu.CompilerParams(vmem_limit_bytes=20 * 1024 * 1024),
        name="apply_factors",
    )(partly, lhs, up, rest)


def body(hamiltonian):
    return update(*factors_kernel(pltpu.with_memory_space_constraint(hamiltonian, pltpu.HBM)))


def solution(mesh):
    return jax.shard_map(
        body, mesh=mesh, in_specs=(P("row", "col"),), out_specs=P("row", "col"), check_vma=False
    )
```

```python
import functools

import jax
import jax.numpy as jnp
from jax import lax
from jax.experimental import pallas as pl
from jax.experimental.pallas import tpu as pltpu
from jax.sharding import PartitionSpec as P

NB = 128
Z, X, C = 8, 4, 8
SH = 64
HS = 32
MESH = pl.DeviceIdType.MESH
HIGH = lax.Precision.HIGHEST
F32 = jnp.float32
BF16 = jnp.bfloat16


def dot(a, b):
    return lax.dot_general(a, b, (((1,), (0,)), ((), ())), precision=HIGH, preferred_element_type=F32)


def dot_nt(a, b):
    return lax.dot_general(a, b, (((1,), (1,)), ((), ())), precision=HIGH, preferred_element_type=F32)


def dot_tn(a, b):
    return lax.dot_general(a, b, (((0,), (0,)), ((), ())), precision=HIGH, preferred_element_type=F32)


def dot_b(a, b, contract):
    return lax.dot_general(a, b, (contract, ((), ())), preferred_element_type=F32)


def halves(value):
    high = value.astype(BF16)
    return high, (value - high.astype(F32)).astype(BF16)


def invert4(m):
    f = 1.0 / (m[0, 0] * m[1, 1] - m[0, 1] * m[0, 1])
    a00, a01, a11 = m[1, 1] * f, -m[0, 1] * f, m[0, 0] * f
    t00, t01 = a00 * m[0, 2] + a01 * m[1, 2], a00 * m[0, 3] + a01 * m[1, 3]
    t10, t11 = a01 * m[0, 2] + a11 * m[1, 2], a01 * m[0, 3] + a11 * m[1, 3]
    s00 = m[2, 2] - (m[0, 2] * t00 + m[1, 2] * t10)
    s01 = m[2, 3] - (m[0, 2] * t01 + m[1, 2] * t11)
    s11 = m[3, 3] - (m[0, 3] * t01 + m[1, 3] * t11)
    g = 1.0 / (s00 * s11 - s01 * s01)
    u00, u01, u11 = s11 * g, -s01 * g, s00 * g
    w00, w01 = -(t00 * u00 + t01 * u01), -(t00 * u01 + t01 * u11)
    w10, w11 = -(t10 * u00 + t11 * u01), -(t10 * u01 + t11 * u11)
    x00 = a00 - (w00 * t00 + w01 * t01)
    x01 = a01 - (w00 * t10 + w01 * t11)
    x11 = a11 - (w10 * t10 + w11 * t11)
    return ((x00, x01, w00, w01), (x01, x11, w10, w11), (w00, w10, u00, u01), (w01, w11, u01, u11))


def sweep_steps(a, groups):
    tile = (8, NB)
    lane = lax.broadcasted_iota(jnp.int32, tile, 1)
    sub = lax.broadcasted_iota(jnp.int32, tile, 0)

    def group(_, a):
        for t in (0, 4):
            rows = [jnp.broadcast_to(a[0, t + i : t + i + 1, :], tile) for i in range(4)]
            block = {
                (i, j): jnp.broadcast_to(rows[i][:, t + j : t + j + 1], tile) for i in range(4) for j in range(i, 4)
            }
            inverse = invert4(block)
            pivot_lane = (lane >= t) & (lane < t + 4)
            rest = jnp.where(pivot_lane[None], 0.0, a)
            new = []
            for i in range(4):
                v = inverse[i]
                n = (v[0] * rows[0] + v[1] * rows[1]) + (v[2] * rows[2] + v[3] * rows[3])
                for j in range(4):
                    n = jnp.where(lane == t + j, v[j], n)
                new.append(n)
                rest = rest - jnp.broadcast_to(a[:, :, t + i : t + i + 1], a.shape) * n[None]
            top = rest[0]
            for i in range(4):
                top = jnp.where(sub == t + i, new[i], top)
            a = jnp.concatenate([top[None], rest[1:]], axis=0)
        a = jnp.concatenate([a[1:], a[:1]], axis=0)
        return pltpu.roll(a, NB - 8, 2)

    return lax.fori_loop(0, groups, group, a.reshape(NB // 8, 8, NB), unroll=True).reshape(NB, NB)


def kernel(
    h_hbm, hv, lhs_ref, up, rest, vs,
    sh, yp, cform, ypr, cr, ur, p2r, part, rsb, ysh, abt, ab,
    pstack, xb, zb, gsum, inv, sc1, sc2, hh, hl, yh, yl, abts, abh,
    h_sem, loc_sem, sc_send, sc_recv, v_send, ra_recv, sp_recv, rp_recv, rx_recv,
    rs_send, rs_recv, p_send, px_recv, pz_recv, pc_recv,
):
    r = lax.axis_index("row")
    c = lax.axis_index("col")
    z = r // X
    x = lax.rem(r, X)
    plane = lax.rem(r, C)
    rel = lax.rem(c - plane + C, C)
    z_up = lax.rem(z + 1, Z)
    z_down = lax.rem(z + Z - 1, Z)
    z_to = jnp.where(rel < 4, z_up, z)
    half = c // 4
    same = lax.rem(z, 2) == half
    z_from = jnp.where(same, z, z_down)

    def remote(src, dst, send, recv, row, col):
        return pltpu.make_async_remote_copy(
            src_ref=src, dst_ref=dst, send_sem=send, recv_sem=recv,
            device_id=(row, col), device_id_type=MESH,
        )

    def landed(rows, sem):
        ref = cform.at[pl.ds(0, rows)]
        remote(ref, ref, sem, sem, r, c).wait_recv()

    def other(d):
        return lax.rem(c + d, C)

    def go(copy):
        copy.start()

    copy_h = pltpu.make_async_copy(h_hbm, hv, h_sem)
    copy_h.start()

    barrier = pltpu.get_barrier_semaphore()

    def greet(row, col):
        pl.semaphore_signal(barrier, inc=1, device_id=(row, col), device_id_type=MESH)

    for d in range(1, C):
        greet(r, other(d))
    for i in range(4):
        greet(z_to * X + i, plane)
        greet(z_from * X + lax.rem(c, X), lax.rem(c + jnp.where(same, 4, 0) + i, C))
    for d in range(1, X):
        greet(z * X + lax.rem(x + d, X), c)
    for d in range(1, Z):
        greet(lax.rem(z + d, Z) * X + x, c)
    pl.semaphore_wait(barrier, 25)

    PV, CV, YV, UV = 0, 1, 2, 3

    def column(v, rows):
        if v == CV:
            return cform.at[rows]
        if v == PV:
            return yp.at[rows, NB : 2 * NB]
        return up.at[rows] if v == UV else yp.at[rows, 0:NB]

    def row(v, rows):
        if v == PV:
            return ypr.at[rows, NB : 2 * NB]
        if v == YV:
            return ypr.at[rows, 0:NB]
        return (cr if v == CV else ur).at[rows]

    def at(start, size):
        return pl.ds(pl.multiple_of(start, 8), size)

    def scatter(v):
        def from_root(d):
            return remote(h_hbm.at[at(SH * other(d), SH), 0:NB], sh.at[v], sc_send.at[v], sc_recv.at[v], r, other(d))

        def own():
            return pltpu.make_async_copy(h_hbm.at[at(SH * c, SH), 0:NB], sh.at[v], loc_sem.at[v])

        @pl.when(c == v)
        def _():
            own().start()
            for d in range(1, C):
                from_root(d).start()

        def finish():
            @pl.when(c == v)
            def _():
                own().wait()
                ref = cform.at[pl.ds(0, (C - 1) * SH)]
                remote(ref, ref, sc_send.at[v], sc_recv.at[v], r, c).wait_send()

            @pl.when(c != v)
            def _():
                from_root(1).wait_recv()

        return finish

    my_off = ((c // 2) * 4 + r // C) * NB + lax.rem(c, 2) * SH

    def distribute(v, shard):
        for i in range(X):
            to = lax.rem(x + i, X)
            part_of = HS * lax.rem(to, 2)
            go(remote(
                shard.at[at(part_of, HS)], column(v, at(my_off + part_of, HS)),
                v_send.at[v], sp_recv.at[v, lax.rem(rel, 4) // 2], z_to * X + to, plane,
            ))
        mine = row(v, at(SH * c, SH))
        for d in range(1, C):
            go(remote(shard, mine, v_send.at[v], ra_recv.at[v], r, other(d)))
        mine[...] = shard[...]

    def wait_rows(v):
        landed((C - 1) * SH, ra_recv.at[v])

    def piece(v, block, i):
        aligned = lax.rem(block, 2) == half
        source = jnp.where(aligned, block, lax.rem(block + Z - 1, Z))
        sender = lax.rem(c + jnp.where(aligned, 4, 0) + i, C)
        off = ((sender // 2) * 4 + source // 2) * NB + lax.rem(sender, 2) * SH + HS * lax.rem(x, 2)
        return column(v, at(off, HS))

    def pass_z(v, s, i, up_way, block):
        k = 0 if up_way else 1
        to = z_up if up_way else z_down
        ref = piece(v, block, i)
        go(remote(ref, ref, v_send.at[v], rp_recv.at[v, k, s - 1, i // 2], to * X + x, c))

    def pass_x(v, i, block):
        to = lax.rem(x + (1 if i < 2 else X - 1), X)
        ref = piece(v, block, i)
        go(remote(ref, ref, v_send.at[v], rx_recv.at[v], z * X + to, c))

    def behind(s, up_way):
        return lax.rem(z - s + Z, Z) if up_way else lax.rem(z + s, Z)

    def ring(v, s):
        for g in (0, 1):
            pair = (2 * g, 2 * g + 1)
            if s == 1:
                landed(2 * HS, sp_recv.at[v, g])
                for i in pair:
                    pass_z(v, 1, i, True, z)
                    pass_z(v, 1, i, False, z)
                for i in pair:
                    pass_x(v, i, z)
                continue
            for up_way in (g == 0, g != 0):
                landed(2 * HS, rp_recv.at[v, 0 if up_way else 1, s - 2, g])
                if s < 4 or up_way == (g == 0):
                    for i in pair:
                        pass_z(v, s, i, up_way, behind(s - 1, up_way))
                for i in pair:
                    pass_x(v, i, behind(s - 1, up_way))

    def ring_last(v):
        for up_way in (True, False):
            g = 0 if up_way else 1
            landed(2 * HS, rp_recv.at[v, g, 3, g])
            for i in (2 * g, 2 * g + 1):
                pass_x(v, i, behind(4, up_way))

    def ring_done(v):
        landed(32 * HS, rx_recv.at[v])

    def reduce_start(q):
        for d in range(1, C):
            go(remote(part.at[q, at(SH * other(d), SH)], rsb.at[q, d - 1], rs_send.at[q], rs_recv.at[q], r, other(d)))

    def reduce_end(q):
        total = part[q, at(SH * c, SH), :]
        landed((C - 1) * SH, rs_recv.at[q])
        for d in range(1, C):
            total = total + rsb[q, d - 1]
        ysh[q] = total

    sizes = (NB, NB, NB, NB, 2 * NB, 2 * NB)

    def sum_start(e):
        m = sizes[e] // C
        xb[e, x, 0:m, :] = pstack[e, at(m * c, m), :]
        for d in range(1, X):
            go(remote(
                pstack.at[e, at(m * c, m)], xb.at[e, x, 0:m], p_send.at[e], px_recv.at[e],
                z * X + lax.rem(x + d, X), c,
            ))

    def sum_z(e):
        m = sizes[e] // C
        landed((X - 1) * m, px_recv.at[e])
        zb[e, z, 0:m, :] = (xb[e, 0, 0:m, :] + xb[e, 1, 0:m, :]) + (xb[e, 2, 0:m, :] + xb[e, 3, 0:m, :])
        for d in range(1, Z):
            ref = zb.at[e, z, 0:m]
            go(remote(ref, ref, p_send.at[e], pz_recv.at[e], lax.rem(z + d, Z) * X + x, c))

    def sum_col(e):
        m = sizes[e] // C
        landed((Z - 1) * m, pz_recv.at[e])
        total = zb[e, 0, 0:m, :]
        for k in range(1, Z):
            total = total + zb[e, k, 0:m, :]
        gsum[e, at(m * c, m), :] = total
        for d in range(1, C):
            ref = gsum.at[e, at(m * c, m)]
            go(remote(ref, ref, p_send.at[e], pc_recv.at[e], r, other(d)))

    def sum_end(e):
        landed((C - 1) * sizes[e] // C, pc_recv.at[e])

    def drain():
        def sent(ref, sem):
            remote(ref, ref, sem, sem, r, c).wait_send()

        for v in range(4):
            sent(yp.at[pl.ds(0, (64 * HS + (C - 1) * SH) // 2)], v_send.at[v])
        for q in range(2):
            sent(cform.at[pl.ds(0, (C - 1) * SH)], rs_send.at[q])
        for e in range(6):
            sent(cform.at[pl.ds(0, (X + Z + C - 3) * sizes[e] // C)], p_send.at[e])

    inner = ((1,), (0,))
    both_last = ((1,), (1,))

    def fold(value):
        return value[:, 0:NB] + value[:, NB : 2 * NB]

    def split_h():
        @pl.loop(0, 8)
        def _(j):
            rows = pl.ds(pl.multiple_of(j * SH, SH), SH)
            hh[rows, :], hl[rows, :] = halves(hv[rows, :])

    def times_h(q):
        @pl.loop(0, 2)
        def _(j):
            rows = pl.ds(pl.multiple_of(j * 2 * NB, 2 * NB), 2 * NB)
            part[q, rows, :] = fold(dot_b(hh[rows, :], vs[...], inner) + dot_b(hl[rows, :], vs[...], inner))

    eye = lax.broadcasted_iota(jnp.int32, (NB, NB), 0) == lax.broadcasted_iota(jnp.int32, (NB, NB), 1)

    def scaled(q, e):
        gram = gsum[e, 0:NB, :]
        diagonal = jnp.where(eye, gram, 0.0)
        sc1[q] = jnp.broadcast_to(lax.rsqrt(jnp.sum(diagonal, axis=0, keepdims=True)), (NB, NB))
        sc2[q] = jnp.broadcast_to(lax.rsqrt(jnp.sum(diagonal, axis=1, keepdims=True)), (NB, NB))
        inv[q] = gram * sc1[q] * sc2[q]

    def sweep(q, groups):
        inv[q] = sweep_steps(inv[q], groups)

    def factors(p, y, k, s, d):
        pk = dot(p * d[0:1, :], k)
        alpha = -2.0 * pk * d[0:1, :]
        beta = dot(4.0 * dot(pk, s) - 2.0 * (y * d[0:1, :]), k) * d[0:1, :]
        return alpha, beta

    def apply_panel1(first, last):
        @pl.loop(first, last)
        def _(k):
            cols = pl.ds(pl.multiple_of(k * 2 * NB, 2 * NB), 2 * NB)
            high, low = yh[cols, :], yl[cols, :]
            hv[:, cols] = hv[:, cols] + (
                dot_b(abh[0], high, both_last) + (dot_b(abh[0], low, both_last) + dot_b(abh[1], high, both_last))
            )

    def rest_of_y2(first, last):
        @pl.loop(first, last)
        def _(k):
            rows = pl.ds(pl.multiple_of(k * 2 * NB, 2 * NB), 2 * NB)
            rest[rows, :] = fold(dot_b(yh[rows, :], abts[...], inner) + dot_b(yl[rows, :], abts[...], inner))

    finish_p = scatter(PV)
    finish_p()

    @pl.when((r == 0) & (c < 2))
    def _():
        sh[PV] = jnp.zeros((SH, NB), F32)

    distribute(PV, sh.at[PV])
    finish_c = scatter(CV)
    ring(PV, 1)
    ring(PV, 2)
    wait_rows(PV)
    p1 = ypr[:, NB : 2 * NB]
    pstack[0, 0:NB, :] = dot_tn(p1, p1)
    sum_start(0)
    ring(PV, 3)
    finish_c()
    distribute(CV, sh.at[CV])
    copy_h.wait()
    split_h()
    ring(PV, 4)
    sum_z(0)
    ring_last(PV)
    ring(CV, 1)
    ring_done(PV)

    @pl.loop(0, 8)
    def _(k):
        rows = pl.ds(pl.multiple_of(k * 2 * NB, 2 * NB), 2 * NB)
        high, low = halves(yp[rows, NB : 2 * NB])
        vs[rows, 0:NB], vs[rows, NB : 2 * NB] = high, low
        yh[rows, NB : 2 * NB], yl[rows, NB : 2 * NB] = high, low

    times_h(0)
    reduce_start(0)
    sum_col(0)
    ring(CV, 2)
    wait_rows(CV)
    pstack[5, 0:NB, :] = dot_tn(cr[...], ypr[:, NB : 2 * NB])
    pstack[5, NB : 2 * NB, :] = jnp.where(r == 1, ypr[0:NB, NB : 2 * NB], 0.0)
    sum_start(5)
    ring(CV, 3)
    reduce_end(0)
    distribute(YV, ysh.at[0])
    ring(CV, 4)
    sum_end(0)
    scaled(0, 0)
    sweep(0, 5)
    sum_z(5)
    ring_last(CV)
    ring(YV, 1)
    wait_rows(YV)
    pstack[1, 0:NB, :] = dot_tn(ypr[:, NB : 2 * NB], ypr[:, 0:NB])
    sum_start(1)
    sweep(0, 4)
    ring(YV, 2)
    sum_z(1)
    sweep(0, 4)
    sum_col(5)
    ring(YV, 3)
    sweep(0, 3)
    sum_col(1)
    ring(YV, 4)
    sum_end(5)
    ring_last(YV)
    sum_end(1)
    k1, d1, e1 = inv[0], sc1[0], sc2[0]
    s1 = gsum[1, 0:NB, :] * d1 * e1
    alpha_b, beta_b = factors(gsum[5, NB : 2 * NB, :], gsum[5, 0:NB, :], k1, s1, d1)
    abt[0:NB, :] = alpha_b.T
    abt[NB : 2 * NB, :] = beta_b.T
    abts[:, 0:NB], abts[:, NB : 2 * NB] = halves(abt[...])
    p2r[...] = cr[...] + dot(ypr[...], abt[...])

    @pl.when(r < 2)
    def _():
        p2r[0:NB, :] = jnp.zeros((NB, NB), F32)

    pstack[2, 0:NB, :] = dot_tn(p2r[...], p2r[...])
    sum_start(2)
    ring_done(CV)
    ring_done(YV)

    @pl.loop(0, 8)
    def _(k):
        rows = pl.ds(pl.multiple_of(k * 2 * NB, 2 * NB), 2 * NB)
        yh[rows, 0:NB], yl[rows, 0:NB] = halves(yp[rows, 0:NB])
        value = cform[rows, :] + fold(dot_b(yh[rows, :], abts[...], inner) + dot_b(yl[rows, :], abts[...], inner))
        sub = lax.broadcasted_iota(jnp.int32, (2 * NB, NB), 0)
        value = jnp.where((sub < NB) & (k == 0) & (c < 2), 0.0, value)
        vs[rows, 0:NB], vs[rows, NB : 2 * NB] = halves(value)

    times_h(1)
    reduce_start(1)
    sum_z(2)
    pstack[4] = dot_tn(ypr[...], p2r[...])
    sum_start(4)
    alpha1, beta1 = factors(ypr[:, NB : 2 * NB], ypr[:, 0:NB], k1, s1, d1)
    abh[0, :, 0:NB], abh[1, :, 0:NB] = halves(alpha1)
    abh[0, :, NB : 2 * NB], abh[1, :, NB : 2 * NB] = halves(beta1)
    apply_panel1(0, 4)
    sum_col(2)
    reduce_end(1)
    distribute(UV, ysh.at[1])
    sum_z(4)
    apply_panel1(4, 6)
    sum_end(2)
    scaled(1, 2)
    sweep(1, 6)
    ring(UV, 1)
    wait_rows(UV)
    pstack[3, 0:NB, :] = dot_tn(p2r[...], ur[...])
    sum_start(3)
    sum_col(4)
    sweep(1, 4)
    ring(UV, 2)
    sum_z(3)
    sweep(1, 6)
    ring(UV, 3)
    sum_end(4)
    t1, t2 = gsum[4, 0:NB, :], gsum[4, NB : 2 * NB, :]
    kt2 = dot(k1, t2 * e1)
    ab[0:NB, :] = -2.0 * kt2 * e1
    ab[NB : 2 * NB, :] = dot(k1, 4.0 * dot(s1, kt2) - 2.0 * (t1 * e1)) * e1
    abts[:, 0:NB], abts[:, NB : 2 * NB] = halves(ab[...])
    rest_of_y2(0, 4)
    sum_col(3)
    ring(UV, 4)
    rest_of_y2(4, 8)
    k2, d2, e2 = inv[1], sc1[1], sc2[1]
    pk2 = dot(p2r[...] * d2[0:1, :], k2)
    lhs_ref[0, :, 0:NB], lhs_ref[1, :, 0:NB] = halves(-2.0 * pk2 * d2[0:1, :])
    ring_last(UV)
    y2 = ur[...] + dot(ypr[...], ab[...])
    apply_panel1(6, 8)
    sum_end(3)
    s2 = (gsum[3, 0:NB, :] + dot_tn(gsum[4], ab[...])) * d2 * e2
    beta2 = dot(4.0 * dot(pk2, s2) - 2.0 * (y2 * d2[0:1, :]), k2) * d2[0:1, :]
    lhs_ref[0, :, NB : 2 * NB], lhs_ref[1, :, NB : 2 * NB] = halves(beta2)
    ring_done(UV)
    drain()


def factors_kernel(hamiltonian):
    rows, cols = hamiltonian.shape
    dma = pltpu.SemaphoreType.DMA
    vmem = pl.BlockSpec(memory_space=pltpu.VMEM)
    return pl.pallas_call(
        kernel,
        out_shape=(
            pltpu.VMEM((rows, cols), F32),
            pltpu.VMEM((2, rows, 2 * NB), BF16),
            pltpu.VMEM((cols, NB), F32),
            pltpu.VMEM((cols, NB), F32),
            pltpu.VMEM((cols, 2 * NB), BF16),
        ),
        in_specs=[pl.BlockSpec(memory_space=pltpu.HBM)],
        out_specs=(vmem, vmem, vmem, vmem, vmem),
        scratch_shapes=[
            pltpu.VMEM((2, SH, NB), F32),
            pltpu.VMEM((cols, 2 * NB), F32),
            pltpu.VMEM((cols, NB), F32),
            pltpu.VMEM((rows, 2 * NB), F32),
            pltpu.VMEM((rows, NB), F32),
            pltpu.VMEM((rows, NB), F32),
            pltpu.VMEM((rows, NB), F32),
            pltpu.VMEM((2, rows, NB), F32),
            pltpu.VMEM((2, C - 1, SH, NB), F32),
            pltpu.VMEM((2, SH, NB), F32),
            pltpu.VMEM((2 * NB, NB), F32),
            pltpu.VMEM((2 * NB, NB), F32),
            pltpu.VMEM((6, 2 * NB, NB), F32),
            pltpu.VMEM((6, X, 2 * NB // C, NB), F32),
            pltpu.VMEM((6, Z, 2 * NB // C, NB), F32),
            pltpu.VMEM((6, 2 * NB, NB), F32),
            pltpu.VMEM((2, NB, NB), F32),
            pltpu.VMEM((2, NB, NB), F32),
            pltpu.VMEM((2, NB, NB), F32),
            pltpu.VMEM((rows, cols), BF16),
            pltpu.VMEM((rows, cols), BF16),
            pltpu.VMEM((cols, 2 * NB), BF16),
            pltpu.VMEM((cols, 2 * NB), BF16),
            pltpu.VMEM((2 * NB, 2 * NB), BF16),
            pltpu.VMEM((2, rows, 2 * NB), BF16),
            dma, dma((2,)), dma((2,)), dma((2,)), dma((4,)), dma((4,)), dma((4, 2)), dma((4, 2, 4, 2)), dma((4,)),
            dma((2,)), dma((2,)), dma((6,)), dma((6,)), dma((6,)), dma((6,)),
        ],
        compiler_params=pltpu.CompilerParams(
            collective_id=0, has_side_effects=True, vmem_limit_bytes=36 * 1024 * 1024
        ),
        name="reflector_factors",
    )(hamiltonian)


def update_kernel(h_ref, lhs_ref, u_ref, rest_ref, vs_ref, out_ref):
    cols = pl.ds(pl.multiple_of(pl.program_id(0) * 2 * NB, 2 * NB), 2 * NB)
    y_high, y_low = halves(u_ref[cols, :] + rest_ref[cols, :])
    high = jnp.concatenate([y_high, vs_ref[cols, 0:NB]], axis=1)
    low = jnp.concatenate([y_low, vs_ref[cols, NB : 2 * NB]], axis=1)
    last = ((1,), (1,))
    out_ref[...] = h_ref[:, cols] + (
        dot_b(lhs_ref[0], high, last) + (dot_b(lhs_ref[0], low, last) + dot_b(lhs_ref[1], high, last))
    )


def update(partly, lhs, u, rest, halves_of_p2):
    rows, cols = partly.shape
    vmem = pl.BlockSpec(memory_space=pltpu.VMEM)
    return pl.pallas_call(
        update_kernel,
        grid=(cols // (2 * NB),),
        out_shape=jax.ShapeDtypeStruct((rows, cols), F32),
        in_specs=[vmem, vmem, vmem, vmem, vmem],
        out_specs=pl.BlockSpec((rows, 2 * NB), lambda i: (0, i)),
        compiler_params=pltpu.CompilerParams(vmem_limit_bytes=20 * 1024 * 1024),
        name="apply_factors",
    )(partly, lhs, u, rest, halves_of_p2)


def body(hamiltonian):
    return update(*factors_kernel(pltpu.with_memory_space_constraint(hamiltonian, pltpu.HBM)))


def solution(mesh):
    return jax.shard_map(
        body, mesh=mesh, in_specs=(P("row", "col"),), out_specs=P("row", "col"), check_vma=False
    )
```

```python
import functools

import jax
import jax.numpy as jnp
from jax import lax
from jax.experimental import pallas as pl
from jax.experimental.pallas import tpu as pltpu
from jax.sharding import PartitionSpec as P

NB = 128
Z, X, C = 8, 4, 8
SH = 64
HS = 32
MESH = pl.DeviceIdType.MESH
HIGH = lax.Precision.HIGHEST
F32 = jnp.float32
BF16 = jnp.bfloat16


def dot(a, b):
    return lax.dot_general(a, b, (((1,), (0,)), ((), ())), precision=HIGH, preferred_element_type=F32)


def dot_nt(a, b):
    return lax.dot_general(a, b, (((1,), (1,)), ((), ())), precision=HIGH, preferred_element_type=F32)


def dot_tn(a, b):
    return lax.dot_general(a, b, (((0,), (0,)), ((), ())), precision=HIGH, preferred_element_type=F32)


def dot_b(a, b, contract):
    return lax.dot_general(a, b, (contract, ((), ())), preferred_element_type=F32)


def halves(value):
    high = value.astype(BF16)
    return high, (value - high.astype(F32)).astype(BF16)


def invert4(m):
    f = 1.0 / (m[0, 0] * m[1, 1] - m[0, 1] * m[0, 1])
    a00, a01, a11 = m[1, 1] * f, -m[0, 1] * f, m[0, 0] * f
    t00, t01 = a00 * m[0, 2] + a01 * m[1, 2], a00 * m[0, 3] + a01 * m[1, 3]
    t10, t11 = a01 * m[0, 2] + a11 * m[1, 2], a01 * m[0, 3] + a11 * m[1, 3]
    s00 = m[2, 2] - (m[0, 2] * t00 + m[1, 2] * t10)
    s01 = m[2, 3] - (m[0, 2] * t01 + m[1, 2] * t11)
    s11 = m[3, 3] - (m[0, 3] * t01 + m[1, 3] * t11)
    g = 1.0 / (s00 * s11 - s01 * s01)
    u00, u01, u11 = s11 * g, -s01 * g, s00 * g
    w00, w01 = -(t00 * u00 + t01 * u01), -(t00 * u01 + t01 * u11)
    w10, w11 = -(t10 * u00 + t11 * u01), -(t10 * u01 + t11 * u11)
    x00 = a00 - (w00 * t00 + w01 * t01)
    x01 = a01 - (w00 * t10 + w01 * t11)
    x11 = a11 - (w10 * t10 + w11 * t11)
    return ((x00, x01, w00, w01), (x01, x11, w10, w11), (w00, w10, u00, u01), (w01, w11, u01, u11))


def sweep_steps(a, groups):
    tile = (8, NB)
    lane = lax.broadcasted_iota(jnp.int32, tile, 1)
    sub = lax.broadcasted_iota(jnp.int32, tile, 0)

    def group(_, a):
        for t in (0, 4):
            rows = [jnp.broadcast_to(a[0, t + i : t + i + 1, :], tile) for i in range(4)]
            block = {
                (i, j): jnp.broadcast_to(rows[i][:, t + j : t + j + 1], tile) for i in range(4) for j in range(i, 4)
            }
            inverse = invert4(block)
            pivot_lane = (lane >= t) & (lane < t + 4)
            rest = jnp.where(pivot_lane[None], 0.0, a)
            new = []
            for i in range(4):
                v = inverse[i]
                n = (v[0] * rows[0] + v[1] * rows[1]) + (v[2] * rows[2] + v[3] * rows[3])
                for j in range(4):
                    n = jnp.where(lane == t + j, v[j], n)
                new.append(n)
                rest = rest - jnp.broadcast_to(a[:, :, t + i : t + i + 1], a.shape) * n[None]
            top = rest[0]
            for i in range(4):
                top = jnp.where(sub == t + i, new[i], top)
            a = jnp.concatenate([top[None], rest[1:]], axis=0)
        a = jnp.concatenate([a[1:], a[:1]], axis=0)
        return pltpu.roll(a, NB - 8, 2)

    return lax.fori_loop(0, groups, group, a.reshape(NB // 8, 8, NB), unroll=True).reshape(NB, NB)


def kernel(
    h_hbm, hv, lhs_ref, up, rest, vs,
    sh, yp, cform, ypr, cr, ur, p2r, part, rsb, ysh, abt, ab,
    pstack, xb, zb, gsum, inv, sc1, sc2, hh, hl, yh, yl, abts, abh,
    h_sem, loc_sem, sc_send, sc_recv, v_send, ra_recv, sp_recv, rp_recv, rx_recv,
    rs_send, rs_recv, p_send, px_recv, pz_recv, pc_recv,
):
    r = lax.axis_index("row")
    c = lax.axis_index("col")
    z = r // X
    x = lax.rem(r, X)
    plane = lax.rem(r, C)
    rel = lax.rem(c - plane + C, C)
    z_up = lax.rem(z + 1, Z)
    z_down = lax.rem(z + Z - 1, Z)
    z_to = jnp.where(rel < 4, z_up, z)
    half = c // 4
    same = lax.rem(z, 2) == half
    z_from = jnp.where(same, z, z_down)

    def remote(src, dst, send, recv, row, col):
        return pltpu.make_async_remote_copy(
            src_ref=src, dst_ref=dst, send_sem=send, recv_sem=recv,
            device_id=(row, col), device_id_type=MESH,
        )

    def landed(rows, sem):
        ref = cform.at[pl.ds(0, rows)]
        remote(ref, ref, sem, sem, r, c).wait_recv()

    def other(d):
        return lax.rem(c + d, C)

    def go(copy):
        copy.start()

    copy_h = pltpu.make_async_copy(h_hbm, hv, h_sem)
    copy_h.start()

    barrier = pltpu.get_barrier_semaphore()

    def greet(row, col):
        pl.semaphore_signal(barrier, inc=1, device_id=(row, col), device_id_type=MESH)

    for d in range(1, C):
        greet(r, other(d))
    for i in range(4):
        greet(z_to * X + i, plane)
        greet(z_from * X + lax.rem(c, X), lax.rem(c + jnp.where(same, 4, 0) + i, C))
    for d in range(1, X):
        greet(z * X + lax.rem(x + d, X), c)
    for d in range(1, Z):
        greet(lax.rem(z + d, Z) * X + x, c)
    pl.semaphore_wait(barrier, 25)

    PV, CV, YV, UV = 0, 1, 2, 3

    def column(v, rows):
        if v == CV:
            return cform.at[rows]
        if v == PV:
            return yp.at[rows, NB : 2 * NB]
        return up.at[rows] if v == UV else yp.at[rows, 0:NB]

    def row(v, rows):
        if v == PV:
            return ypr.at[rows, NB : 2 * NB]
        if v == YV:
            return ypr.at[rows, 0:NB]
        return (cr if v == CV else ur).at[rows]

    def at(start, size):
        return pl.ds(pl.multiple_of(start, 8), size)

    def scatter(v):
        def from_root(d):
            return remote(h_hbm.at[at(SH * other(d), SH), 0:NB], sh.at[v], sc_send.at[v], sc_recv.at[v], r, other(d))

        def own():
            return pltpu.make_async_copy(h_hbm.at[at(SH * c, SH), 0:NB], sh.at[v], loc_sem.at[v])

        @pl.when(c == v)
        def _():
            own().start()
            for d in range(1, C):
                from_root(d).start()

        def finish():
            @pl.when(c == v)
            def _():
                own().wait()
                ref = cform.at[pl.ds(0, (C - 1) * SH)]
                remote(ref, ref, sc_send.at[v], sc_recv.at[v], r, c).wait_send()

            @pl.when(c != v)
            def _():
                from_root(1).wait_recv()

        return finish

    my_off = ((c // 2) * 4 + r // C) * NB + lax.rem(c, 2) * SH

    def distribute(v, shard):
        for i in range(X):
            to = lax.rem(x + i, X)
            part_of = HS * lax.rem(to, 2)
            go(remote(
                shard.at[at(part_of, HS)], column(v, at(my_off + part_of, HS)),
                v_send.at[v], sp_recv.at[v, lax.rem(rel, 4) // 2], z_to * X + to, plane,
            ))
        mine = row(v, at(SH * c, SH))
        for d in range(1, C):
            go(remote(shard, mine, v_send.at[v], ra_recv.at[v], r, other(d)))
        mine[...] = shard[...]

    def wait_rows(v):
        landed((C - 1) * SH, ra_recv.at[v])

    def piece(v, block, i):
        aligned = lax.rem(block, 2) == half
        source = jnp.where(aligned, block, lax.rem(block + Z - 1, Z))
        sender = lax.rem(c + jnp.where(aligned, 4, 0) + i, C)
        off = ((sender // 2) * 4 + source // 2) * NB + lax.rem(sender, 2) * SH + HS * lax.rem(x, 2)
        return column(v, at(off, HS))

    def pass_z(v, s, i, up_way, block):
        k = 0 if up_way else 1
        to = z_up if up_way else z_down
        ref = piece(v, block, i)
        go(remote(ref, ref, v_send.at[v], rp_recv.at[v, k, s - 1, i // 2], to * X + x, c))

    def pass_x(v, i, block):
        to = lax.rem(x + (1 if i < 2 else X - 1), X)
        ref = piece(v, block, i)
        go(remote(ref, ref, v_send.at[v], rx_recv.at[v], z * X + to, c))

    def behind(s, up_way):
        return lax.rem(z - s + Z, Z) if up_way else lax.rem(z + s, Z)

    def ring(v, s):
        for g in (0, 1):
            pair = (2 * g, 2 * g + 1)
            if s == 1:
                landed(2 * HS, sp_recv.at[v, g])
                for i in pair:
                    pass_z(v, 1, i, True, z)
                    pass_z(v, 1, i, False, z)
                for i in pair:
                    pass_x(v, i, z)
                continue
            for up_way in (g == 0, g != 0):
                landed(2 * HS, rp_recv.at[v, 0 if up_way else 1, s - 2, g])
                if s < 4 or up_way == (g == 0):
                    for i in pair:
                        pass_z(v, s, i, up_way, behind(s - 1, up_way))
                for i in pair:
                    pass_x(v, i, behind(s - 1, up_way))

    def ring_last(v):
        for up_way in (True, False):
            g = 0 if up_way else 1
            landed(2 * HS, rp_recv.at[v, g, 3, g])
            for i in (2 * g, 2 * g + 1):
                pass_x(v, i, behind(4, up_way))

    def ring_done(v):
        landed(32 * HS, rx_recv.at[v])

    def reduce_start(q):
        for d in range(1, C):
            go(remote(part.at[q, at(SH * other(d), SH)], rsb.at[q, d - 1], rs_send.at[q], rs_recv.at[q], r, other(d)))

    def reduce_end(q):
        total = part[q, at(SH * c, SH), :]
        landed((C - 1) * SH, rs_recv.at[q])
        for d in range(1, C):
            total = total + rsb[q, d - 1]
        ysh[q] = total

    sizes = (NB, NB, NB, NB, 2 * NB, 2 * NB)

    def sum_start(e):
        m = sizes[e] // C
        xb[e, x, 0:m, :] = pstack[e, at(m * c, m), :]
        for d in range(1, X):
            go(remote(
                pstack.at[e, at(m * c, m)], xb.at[e, x, 0:m], p_send.at[e], px_recv.at[e],
                z * X + lax.rem(x + d, X), c,
            ))

    def sum_z(e):
        m = sizes[e] // C
        landed((X - 1) * m, px_recv.at[e])
        zb[e, z, 0:m, :] = (xb[e, 0, 0:m, :] + xb[e, 1, 0:m, :]) + (xb[e, 2, 0:m, :] + xb[e, 3, 0:m, :])
        for d in range(1, Z):
            ref = zb.at[e, z, 0:m]
            go(remote(ref, ref, p_send.at[e], pz_recv.at[e], lax.rem(z + d, Z) * X + x, c))

    def sum_col(e):
        m = sizes[e] // C
        landed((Z - 1) * m, pz_recv.at[e])
        total = zb[e, 0, 0:m, :]
        for k in range(1, Z):
            total = total + zb[e, k, 0:m, :]
        gsum[e, at(m * c, m), :] = total
        for d in range(1, C):
            ref = gsum.at[e, at(m * c, m)]
            go(remote(ref, ref, p_send.at[e], pc_recv.at[e], r, other(d)))

    def sum_end(e):
        landed((C - 1) * sizes[e] // C, pc_recv.at[e])

    def drain():
        def sent(ref, sem):
            remote(ref, ref, sem, sem, r, c).wait_send()

        for v in range(4):
            sent(yp.at[pl.ds(0, (64 * HS + (C - 1) * SH) // 2)], v_send.at[v])
        for q in range(2):
            sent(cform.at[pl.ds(0, (C - 1) * SH)], rs_send.at[q])
        for e in range(6):
            sent(cform.at[pl.ds(0, (X + Z + C - 3) * sizes[e] // C)], p_send.at[e])

    inner = ((1,), (0,))
    both_last = ((1,), (1,))

    def fold(value):
        return value[:, 0:NB] + value[:, NB : 2 * NB]

    def split_h():
        @pl.loop(0, 8)
        def _(j):
            rows = pl.ds(pl.multiple_of(j * SH, SH), SH)
            hh[rows, :], hl[rows, :] = halves(hv[rows, :])

    def times_h(q):
        @pl.loop(0, 2)
        def _(j):
            rows = pl.ds(pl.multiple_of(j * 2 * NB, 2 * NB), 2 * NB)
            part[q, rows, :] = fold(dot_b(hh[rows, :], vs[...], inner) + dot_b(hl[rows, :], vs[...], inner))

    eye = lax.broadcasted_iota(jnp.int32, (NB, NB), 0) == lax.broadcasted_iota(jnp.int32, (NB, NB), 1)

    def scaled(q, e):
        gram = gsum[e, 0:NB, :]
        diagonal = jnp.where(eye, gram, 0.0)
        sc1[q] = jnp.broadcast_to(lax.rsqrt(jnp.sum(diagonal, axis=0, keepdims=True)), (NB, NB))
        sc2[q] = jnp.broadcast_to(lax.rsqrt(jnp.sum(diagonal, axis=1, keepdims=True)), (NB, NB))
        inv[q] = gram * sc1[q] * sc2[q]

    def sweep(q, groups):
        inv[q] = sweep_steps(inv[q], groups)

    def factors(p, y, k, s, d):
        pk = dot(p * d[0:1, :], k)
        alpha = -2.0 * pk * d[0:1, :]
        beta = dot(4.0 * dot(pk, s) - 2.0 * (y * d[0:1, :]), k) * d[0:1, :]
        return alpha, beta

    def apply_panel1(first, last):
        @pl.loop(first, last)
        def _(k):
            cols = pl.ds(pl.multiple_of(k * 2 * NB, 2 * NB), 2 * NB)
            high, low = yh[cols, :], yl[cols, :]
            hv[:, cols] = hv[:, cols] + (
                dot_b(abh[0], high, both_last) + (dot_b(abh[0], low, both_last) + dot_b(abh[1], high, both_last))
            )

    def rest_of_y2(first, last):
        @pl.loop(first, last)
        def _(k):
            rows = pl.ds(pl.multiple_of(k * 2 * NB, 2 * NB), 2 * NB)
            rest[rows, :] = fold(dot_b(yh[rows, :], abts[...], inner) + dot_b(yl[rows, :], abts[...], inner))

    finish_p = scatter(PV)
    finish_p()

    @pl.when((r == 0) & (c < 2))
    def _():
        sh[PV] = jnp.zeros((SH, NB), F32)

    distribute(PV, sh.at[PV])
    finish_c = scatter(CV)
    ring(PV, 1)
    ring(PV, 2)
    wait_rows(PV)
    p1 = ypr[:, NB : 2 * NB]
    pstack[0, 0:NB, :] = dot_tn(p1, p1)
    sum_start(0)
    ring(PV, 3)
    finish_c()
    distribute(CV, sh.at[CV])
    copy_h.wait()
    split_h()
    ring(PV, 4)
    sum_z(0)
    ring_last(PV)
    ring(CV, 1)
    ring_done(PV)

    @pl.loop(0, 8)
    def _(k):
        rows = pl.ds(pl.multiple_of(k * 2 * NB, 2 * NB), 2 * NB)
        high, low = halves(yp[rows, NB : 2 * NB])
        vs[rows, 0:NB], vs[rows, NB : 2 * NB] = high, low
        yh[rows, NB : 2 * NB], yl[rows, NB : 2 * NB] = high, low

    times_h(0)
    reduce_start(0)
    sum_col(0)
    ring(CV, 2)
    wait_rows(CV)
    pstack[5, 0:NB, :] = dot_tn(cr[...], ypr[:, NB : 2 * NB])
    pstack[5, NB : 2 * NB, :] = jnp.where(r == 1, ypr[0:NB, NB : 2 * NB], 0.0)
    sum_start(5)
    ring(CV, 3)
    reduce_end(0)
    distribute(YV, ysh.at[0])
    ring(CV, 4)
    sum_end(0)
    scaled(0, 0)
    sweep(0, 5)
    sum_z(5)
    ring_last(CV)
    ring(YV, 1)
    wait_rows(YV)
    pstack[1, 0:NB, :] = dot_tn(ypr[:, NB : 2 * NB], ypr[:, 0:NB])
    sum_start(1)
    sweep(0, 4)
    ring(YV, 2)
    sum_z(1)
    sweep(0, 4)
    sum_col(5)
    ring(YV, 3)
    sweep(0, 3)
    sum_col(1)
    ring(YV, 4)
    sum_end(5)
    ring_last(YV)
    sum_end(1)
    k1, d1, e1 = inv[0], sc1[0], sc2[0]
    s1 = gsum[1, 0:NB, :] * d1 * e1
    alpha_b, beta_b = factors(gsum[5, NB : 2 * NB, :], gsum[5, 0:NB, :], k1, s1, d1)
    abt[0:NB, :] = alpha_b.T
    abt[NB : 2 * NB, :] = beta_b.T
    abts[:, 0:NB], abts[:, NB : 2 * NB] = halves(abt[...])
    p2r[...] = cr[...] + dot(ypr[...], abt[...])

    @pl.when(r < 2)
    def _():
        p2r[0:NB, :] = jnp.zeros((NB, NB), F32)

    pstack[2, 0:NB, :] = dot_tn(p2r[...], p2r[...])
    sum_start(2)
    ring_done(CV)
    ring_done(YV)

    @pl.loop(0, 8)
    def _(k):
        rows = pl.ds(pl.multiple_of(k * 2 * NB, 2 * NB), 2 * NB)
        yh[rows, 0:NB], yl[rows, 0:NB] = halves(yp[rows, 0:NB])
        value = cform[rows, :] + fold(dot_b(yh[rows, :], abts[...], inner) + dot_b(yl[rows, :], abts[...], inner))
        sub = lax.broadcasted_iota(jnp.int32, (2 * NB, NB), 0)
        value = jnp.where((sub < NB) & (k == 0) & (c < 2), 0.0, value)
        vs[rows, 0:NB], vs[rows, NB : 2 * NB] = halves(value)

    times_h(1)
    reduce_start(1)
    sum_z(2)
    pstack[4] = dot_tn(ypr[...], p2r[...])
    sum_start(4)
    alpha1, beta1 = factors(ypr[:, NB : 2 * NB], ypr[:, 0:NB], k1, s1, d1)
    abh[0, :, 0:NB], abh[1, :, 0:NB] = halves(alpha1)
    abh[0, :, NB : 2 * NB], abh[1, :, NB : 2 * NB] = halves(beta1)
    apply_panel1(0, 4)
    sum_col(2)
    reduce_end(1)
    distribute(UV, ysh.at[1])
    sum_z(4)
    apply_panel1(4, 6)
    sum_end(2)
    scaled(1, 2)
    sweep(1, 6)
    ring(UV, 1)
    wait_rows(UV)
    pstack[3, 0:NB, :] = dot_tn(p2r[...], ur[...])
    sum_start(3)
    sum_col(4)
    sweep(1, 4)
    ring(UV, 2)
    sum_z(3)
    sweep(1, 6)
    ring(UV, 3)
    sum_end(4)
    t1, t2 = gsum[4, 0:NB, :], gsum[4, NB : 2 * NB, :]
    kt2 = dot(k1, t2 * e1)
    ab[0:NB, :] = -2.0 * kt2 * e1
    ab[NB : 2 * NB, :] = dot(k1, 4.0 * dot(s1, kt2) - 2.0 * (t1 * e1)) * e1
    abts[:, 0:NB], abts[:, NB : 2 * NB] = halves(ab[...])
    rest_of_y2(0, 4)
    sum_col(3)
    ring(UV, 4)
    rest_of_y2(4, 8)
    k2, d2, e2 = inv[1], sc1[1], sc2[1]
    pk2 = dot(p2r[...] * d2[0:1, :], k2)
    lhs_ref[0, :, 0:NB], lhs_ref[1, :, 0:NB] = halves(-2.0 * pk2 * d2[0:1, :])
    ring_last(UV)
    y2 = ur[...] + dot(ypr[...], ab[...])
    apply_panel1(6, 8)
    sum_end(3)
    s2 = (gsum[3, 0:NB, :] + dot_tn(gsum[4], ab[...])) * d2 * e2
    beta2 = dot(4.0 * dot(pk2, s2) - 2.0 * (y2 * d2[0:1, :]), k2) * d2[0:1, :]
    lhs_ref[0, :, NB : 2 * NB], lhs_ref[1, :, NB : 2 * NB] = halves(beta2)
    ring_done(UV)
    drain()


def factors_kernel(hamiltonian):
    rows, cols = hamiltonian.shape
    dma = pltpu.SemaphoreType.DMA
    vmem = pl.BlockSpec(memory_space=pltpu.VMEM)
    return pl.pallas_call(
        kernel,
        out_shape=(
            pltpu.VMEM((rows, cols), F32),
            pltpu.VMEM((2, rows, 2 * NB), BF16),
            pltpu.VMEM((cols, NB), F32),
            pltpu.VMEM((cols, NB), F32),
            pltpu.VMEM((cols, 2 * NB), BF16),
        ),
        in_specs=[pl.BlockSpec(memory_space=pltpu.HBM)],
        out_specs=(vmem, vmem, vmem, vmem, vmem),
        scratch_shapes=[
            pltpu.VMEM((2, SH, NB), F32),
            pltpu.VMEM((cols, 2 * NB), F32),
            pltpu.VMEM((cols, NB), F32),
            pltpu.VMEM((rows, 2 * NB), F32),
            pltpu.VMEM((rows, NB), F32),
            pltpu.VMEM((rows, NB), F32),
            pltpu.VMEM((rows, NB), F32),
            pltpu.VMEM((2, rows, NB), F32),
            pltpu.VMEM((2, C - 1, SH, NB), F32),
            pltpu.VMEM((2, SH, NB), F32),
            pltpu.VMEM((2 * NB, NB), F32),
            pltpu.VMEM((2 * NB, NB), F32),
            pltpu.VMEM((6, 2 * NB, NB), F32),
            pltpu.VMEM((6, X, 2 * NB // C, NB), F32),
            pltpu.VMEM((6, Z, 2 * NB // C, NB), F32),
            pltpu.VMEM((6, 2 * NB, NB), F32),
            pltpu.VMEM((2, NB, NB), F32),
            pltpu.VMEM((2, NB, NB), F32),
            pltpu.VMEM((2, NB, NB), F32),
            pltpu.VMEM((rows, cols), BF16),
            pltpu.VMEM((rows, cols), BF16),
            pltpu.VMEM((cols, 2 * NB), BF16),
            pltpu.VMEM((cols, 2 * NB), BF16),
            pltpu.VMEM((2 * NB, 2 * NB), BF16),
            pltpu.VMEM((2, rows, 2 * NB), BF16),
            dma, dma((2,)), dma((2,)), dma((2,)), dma((4,)), dma((4,)), dma((4, 2)), dma((4, 2, 4, 2)), dma((4,)),
            dma((2,)), dma((2,)), dma((6,)), dma((6,)), dma((6,)), dma((6,)),
        ],
        compiler_params=pltpu.CompilerParams(
            collective_id=0, has_side_effects=True, vmem_limit_bytes=36 * 1024 * 1024
        ),
        name="reflector_factors",
    )(hamiltonian)


def update_kernel(h_ref, lhs_ref, u_ref, rest_ref, vs_ref, out_ref):
    cols = pl.ds(pl.multiple_of(pl.program_id(0) * 4 * NB, 4 * NB), 4 * NB)
    y_high, y_low = halves(u_ref[cols, :] + rest_ref[cols, :])
    high = jnp.concatenate([y_high, vs_ref[cols, 0:NB]], axis=1)
    low = jnp.concatenate([y_low, vs_ref[cols, NB : 2 * NB]], axis=1)
    last = ((1,), (1,))
    out_ref[...] = h_ref[:, cols] + (
        dot_b(lhs_ref[0], high, last) + (dot_b(lhs_ref[0], low, last) + dot_b(lhs_ref[1], high, last))
    )


def update(partly, lhs, u, rest, halves_of_p2):
    rows, cols = partly.shape
    vmem = pl.BlockSpec(memory_space=pltpu.VMEM)
    return pl.pallas_call(
        update_kernel,
        grid=(cols // (4 * NB),),
        out_shape=jax.ShapeDtypeStruct((rows, cols), F32),
        in_specs=[vmem, vmem, vmem, vmem, vmem],
        out_specs=pl.BlockSpec((rows, 4 * NB), lambda i: (0, i)),
        compiler_params=pltpu.CompilerParams(vmem_limit_bytes=20 * 1024 * 1024),
        name="apply_factors",
    )(partly, lhs, u, rest, halves_of_p2)


def body(hamiltonian):
    return update(*factors_kernel(pltpu.with_memory_space_constraint(hamiltonian, pltpu.HBM)))


def solution(mesh):
    return jax.shard_map(
        body, mesh=mesh, in_specs=(P("row", "col"),), out_specs=P("row", "col"), check_vma=False
    )
```
